32 devices in a mesh: tm: 8 (over z, x), lon: 4 (over y, core).
Axes of the slice: x: 2, y: 2, z: 4, core: 2. Of those that a mesh axis runs over, the one named last changes fastest.
Arguments:
- start: float32 [3, 128, 512], P(None, 'lon'), may hold values from -6 to 6
- depth: float32 [128, 512], P('lon'), may hold values from 0.5 to 1.5
Outputs:
- ends: float32 [8, 3, 128, 512], P('tm', None, 'lon')
The draws below stay inside these ranges and needn't reach their ends.
All inputs are finite; a program needn't handle non-finite values.
Results may differ from the reference program's by a relative error of at most 0.00002.
Values sent between devices are 32-bit elements; how exact they have to be, the bound alone decides.
No kernel may reach another device: no remote copies, remote signals or barrier semaphores. Data moves between devices by JAX's collectives and lax.ppermute only.
A program may use at most 64 MiB of HBM per device.

```python
import math
import jax
import jax.numpy as jnp
from jax import lax

NLAT = 512
STEPS = 3
ROUNDS = 2
TSLICES = 8
NLON = 128


def levels(stream_key, extent, split, least, high):
    def one(dim, shards_of):
        heights = jax.random.uniform(jax.random.fold_in(jax.random.fold_in(stream_key, 6), dim), (shards_of,), jnp.float32, least / len(split), high / len(split))
        return jnp.repeat(jnp.exp(heights), extent[dim] // shards_of).reshape((-1,) + (1,) * (len(extent) - dim - 1))

    loudness = one(*split[0])
    for cut in split[1:]:
        loudness = loudness * one(*cut)
    return loudness


def bell_draw(rng, extent, scale, most, pieces=(), kind=jnp.bfloat16):
    factor_of = levels(rng, extent, pieces, -0.22, 0.18) if pieces else 1.0
    array = jax.random.normal(rng, extent, jnp.float32) * scale * factor_of
    return jnp.minimum(jnp.maximum(array, -most), most).astype(kind)


def setup_inputs(seed: int = 0) -> dict:
    keys = jax.random.split(jax.random.key(seed), 3)
    start = bell_draw(keys[0], (3, NLON, NLAT), 1.0, 6.0, ((1, 4),), jnp.float32)
    depth = jnp.clip(0.5 + 1.0 * jax.random.uniform(keys[1], (NLON, NLAT), jnp.float32) ** levels(keys[1], (NLON, NLAT), ((0, 4),), -0.2, 0.2), 0.5, 1.5)
    return {"start": start, "depth": depth}


LAT_LIMIT = 1.2
COURANT = 1.2
DEPTH_MAX = 1.5
GRAVITY = 1.0
TURN_RATE = 0.15

def grid_constants(lon_cells, lat_cells):
    latitude = -LAT_LIMIT + (jnp.arange(lat_cells, dtype=jnp.float32) + 0.5) * (2.0 * LAT_LIMIT / lat_cells)
    cosine = jnp.cos(latitude)
    north_spacing = 2.0 * LAT_LIMIT / lat_cells
    east_spacing = cosine * (2.0 * math.pi / lon_cells)
    narrowest = math.cos(LAT_LIMIT - LAT_LIMIT / lat_cells) * 2.0 * math.pi / lon_cells
    time_step = COURANT / (math.sqrt(DEPTH_MAX * GRAVITY) * math.sqrt(1.0 / narrowest ** 2 + 1.0 / north_spacing ** 2))
    coriolis = TURN_RATE * jnp.sin(latitude) / time_step
    turning = coriolis * (STEPS * time_step)
    return (cosine, east_spacing, north_spacing, time_step, coriolis, turning)

def north_diff(values):
    padded = jnp.pad(values, ((0, 0), (1, 1)))
    return padded[:, 2:] - padded[:, :-2]

def advance(state_wide, depth_wide, consts):
    cosine, east_spacing, north_spacing, time_step, coriolis, turning = consts
    height = state_wide[0]
    zonal = state_wide[1]
    merid = state_wide[2]
    flux_east = depth_wide * zonal
    flux_north = depth_wide[1:-1] * merid[1:-1] * cosine
    diverge = (flux_east[2:] - flux_east[:-2]) / (2.0 * east_spacing) + north_diff(flux_north) / (2.0 * north_spacing * cosine)
    height_new = height[1:-1] - time_step * diverge
    zonal_new = zonal[2:-2] + time_step * (coriolis * merid[2:-2] - GRAVITY * (height_new[2:] - height_new[:-2]) / (2.0 * east_spacing))
    merid_new = merid[2:-2] + time_step * (-coriolis * zonal_new - GRAVITY * north_diff(height_new[1:-1]) / (2.0 * north_spacing))
    return jnp.stack([height_new[1:-1], zonal_new, merid_new])

def rotate(state, angle):
    cos_angle = jnp.cos(angle)
    sin_angle = jnp.sin(angle)
    zonal = state[..., 1, :, :]
    merid = state[..., 2, :, :]
    return jnp.stack([state[..., 0, :, :], zonal * cos_angle + merid * sin_angle, merid * cos_angle - zonal * sin_angle], axis=-3)

def reference(start, depth):
    consts = grid_constants(NLON, NLAT)
    turning = consts[5]
    depth_wide = jnp.concatenate([depth[-2:], depth, depth[:2]], axis=0)

    def fine(state):
        for turn_index in range(STEPS):
            padded = jnp.concatenate([state[:, -2:], state, state[:, :2]], axis=1)
            state = advance(padded, depth_wide, consts)
        return state
    numbers = jnp.arange(TSLICES, dtype=jnp.float32)
    guesses = lax.map(lambda number: rotate(start, number * turning), numbers)

    def chain(carry, piece):
        following = rotate(carry, turning) + piece
        return (following, following)
    ends = guesses
    for round_index in range(ROUNDS):
        fines = lax.map(fine, guesses)
        correct = fines - rotate(guesses, turning)
        last_state, ends = lax.scan(chain, start, correct)
        guesses = jnp.concatenate([start[None], ends[:-1]], axis=0)
    return ends
```

```python
import math

import jax
import jax.numpy as jnp
import numpy as np
from jax import lax
from jax.experimental import pallas as pl
from jax.experimental.pallas import tpu as pltpu
from jax.sharding import PartitionSpec as P

STEPS = 3
ROUNDS = 2
LAT_LIMIT = 1.2
COURANT = 1.2
DEPTH_MAX = 1.5
GRAVITY = 1.0
TURN_RATE = 0.15

HALO = 2 * STEPS * ROUNDS
ROWS = 8
LANES = 128
VMEM_LIMIT = 16 << 20

EAST, POLE, DIVERGE, SPIN_U, SPIN_V, GRAD_E, GRAD_N, TURN_C, TURN_U, TURN_V, EAST_INV, POLE_INV = range(12)


def lat_table(lon_cells, lat_cells):
    latitude = -LAT_LIMIT + (np.arange(lat_cells) + 0.5) * (2.0 * LAT_LIMIT / lat_cells)
    cosine = np.cos(latitude)
    north_spacing = 2.0 * LAT_LIMIT / lat_cells
    east_spacing = cosine * (2.0 * math.pi / lon_cells)
    narrowest = math.cos(LAT_LIMIT - LAT_LIMIT / lat_cells) * 2.0 * math.pi / lon_cells
    time_step = COURANT / (
        math.sqrt(DEPTH_MAX * GRAVITY) * math.sqrt(1.0 / narrowest**2 + 1.0 / north_spacing**2)
    )
    spin = TURN_RATE * np.sin(latitude)
    turning = spin * STEPS
    east = time_step / (2.0 * east_spacing)
    north = time_step / (2.0 * north_spacing)
    rows = [None] * 12
    rows[EAST] = east
    rows[POLE] = cosine
    rows[DIVERGE] = north / cosine
    rows[SPIN_U] = spin * east / cosine
    rows[SPIN_V] = spin * cosine / east
    rows[GRAD_E] = GRAVITY * east
    rows[GRAD_N] = GRAVITY * north + 0.0 * cosine
    rows[TURN_C] = np.cos(turning)
    rows[TURN_U] = np.sin(turning) * east / cosine
    rows[TURN_V] = np.sin(turning) * cosine / east
    rows[EAST_INV] = 1.0 / east
    rows[POLE_INV] = 1.0 / cosine
    table = np.stack(rows).astype(np.float32)
    return np.broadcast_to(table[:, None, :], (12, ROWS, lat_cells)).copy()


def windows(low, high):
    starts = list(range(low, high - ROWS + 1, ROWS))
    if starts[-1] + ROWS < high:
        starts.append(high - ROWS)
    return starts


def kernel(cells, tiles, start, depth, left, right, table, ends, *scratch):
    (s_h, u_a, u_b, v_h, v_a, v_b, w_h, w_a, w_b, grad_e, grad_n, inverse) = scratch[:12]
    temps1 = scratch[12:18]
    temps2 = scratch[18:24]
    wide = cells + 2 * HALO
    number = lax.axis_index("tm")
    lane = lax.broadcasted_iota(jnp.int32, (ROWS, LANES), 1)
    first = lane == 0
    last = lane == LANES - 1
    zero = jnp.zeros((ROWS, LANES), jnp.float32)

    def const(row, t):
        return table[row, :, t * LANES : (t + 1) * LANES]

    def at(ref, t, row):
        return ref[t, row : row + ROWS, :]

    def put(ref, t, row, value):
        ref[t, row : row + ROWS, :] = value

    def north_diff(parts):
        out = []
        for t in range(tiles):
            above = parts[t + 1] if t + 1 < tiles else zero
            below = parts[t - 1] if t > 0 else zero
            up = pltpu.roll(jnp.where(first, above, parts[t]), LANES - 1, 1)
            down = pltpu.roll(jnp.where(last, below, parts[t]), 1, 1)
            out.append(up - down)
        return out

    def load_block(field_of, depth_of, count, base):
        for row in windows(0, count):
            for t in range(tiles):
                h = depth_of(row, t)
                he = h * const(EAST, t)
                hp = h * const(POLE, t)
                put(s_h, t, base + row, field_of(0, row, t))
                put(u_a, t, base + row, field_of(1, row, t) * he)
                put(u_b, t, base + row, field_of(2, row, t) * hp)
                put(grad_e, t, base + row, he * const(GRAD_E, t))
                put(grad_n, t, base + row, hp * const(GRAD_N, t))

    def part(ref, *lead):
        return lambda row, t: ref[(*lead, slice(row, row + ROWS), slice(t * LANES, (t + 1) * LANES))]

    load_block(lambda f, r, t: part(start, f)(r, t), part(depth), cells, HALO)
    load_block(lambda f, r, t: part(left, f)(r, t), part(left, 3), HALO, 0)
    load_block(lambda f, r, t: part(right, f)(r, t), part(right, 3), HALO, HALO + cells)

    def fine(source, low, high, temps):
        state = source
        for step in range(STEPS):
            height, alpha, beta = state
            new = temps[3 * (step % 2) : 3 * (step % 2) + 3]
            new_h, new_a, new_b = new
            for row in windows(low + 1, high - 1):
                flux = north_diff([at(beta, t, row) for t in range(tiles)])
                for t in range(tiles):
                    value = at(height, t, row) - (at(alpha, t, row + 1) - at(alpha, t, row - 1))
                    put(new_h, t, row, value - const(DIVERGE, t) * flux[t])
            for row in windows(low + 2, high - 2):
                slope = north_diff([at(new_h, t, row) for t in range(tiles)])
                for t in range(tiles):
                    b = at(beta, t, row)
                    east = at(new_h, t, row + 1) - at(new_h, t, row - 1)
                    a = at(alpha, t, row) + const(SPIN_U, t) * b - at(grad_e, t, row) * east
                    put(new_a, t, row, a)
                    b = b - const(SPIN_V, t) * a - at(grad_n, t, row) * slope[t]
                    put(new_b, t, row, b)
            state = new
            low, high = low + 2, high - 2
        return state

    def turn(a, b, t):
        c = const(TURN_C, t)
        return c * a + const(TURN_U, t) * b, c * b - const(TURN_V, t) * a

    reach = 2 * STEPS

    def round_one(first_time):
        x_h, x_a, x_b = fine((s_h, u_a, u_b), 0, wide, temps1)
        for row in windows(reach, wide - reach):
            for t in range(tiles):
                xh, xa, xb = at(x_h, t, row), at(x_a, t, row), at(x_b, t, row)
                if not first_time:
                    xh = xh + (at(v_h, t, row) - at(s_h, t, row))
                    a, b = turn(
                        at(v_a, t, row) - at(u_a, t, row), at(v_b, t, row) - at(u_b, t, row), t
                    )
                    xa, xb = xa + a, xb + b
                put(n_h, t, row, xh)
                put(n_a, t, row, xa)
                put(n_b, t, row, xb)

    n_h, n_a, n_b = scratch[24:27]

    def turn_guess():
        for row in range(0, wide, ROWS):
            for t in range(tiles):
                a, b = turn(at(u_a, t, row), at(u_b, t, row), t)
                put(u_a, t, row, a)
                put(u_b, t, row, b)

    def move(low, high, targets):
        for row in windows(low, high):
            for t in range(tiles):
                for source, target in zip((n_h, n_a, n_b), targets):
                    put(target, t, row, at(source, t, row))

    def round_two():
        y = fine((v_h, v_a, v_b), reach, wide - reach, temps2)
        for row in windows(HALO, HALO + cells):
            for t in range(tiles):
                yh, ya, yb = (at(ref, t, row) for ref in y)
                yh = yh + (at(w_h, t, row) - at(v_h, t, row))
                a, b = turn(at(w_a, t, row) - at(v_a, t, row), at(w_b, t, row) - at(v_b, t, row), t)
                put(w_h, t, row, yh)
                put(w_a, t, row, ya + a)
                put(w_b, t, row, yb + b)

    round_one(True)
    move(reach, wide - reach, (v_h, v_a, v_b))
    move(HALO, HALO + cells, (w_h, w_a, w_b))

    def both(index, carry):
        turn_guess()
        round_one(False)
        round_two()
        move(reach, wide - reach, (v_h, v_a, v_b))
        return carry

    lax.fori_loop(1, number, both, 0)

    @pl.when(number > 0)
    def _():
        round_two()

    for row in windows(0, cells):
        for t in range(tiles):
            span = (slice(row, row + ROWS), slice(t * LANES, (t + 1) * LANES))
            over = 1.0 / depth[span]
            ends[(0, 0, *span)] = at(w_h, t, HALO + row)
            ends[(0, 1, *span)] = at(w_a, t, HALO + row) * (over * const(EAST_INV, t))
            ends[(0, 2, *span)] = at(w_b, t, HALO + row) * (over * const(POLE_INV, t))


def body(start, depth):
    count = lax.axis_size("lon")
    _, cells, lat_cells = start.shape
    tiles = lat_cells // LANES
    table = lat_table(cells * count, lat_cells)
    both = jnp.concatenate([start, depth[None]], axis=0)
    left = lax.ppermute(both[:, cells - HALO :], "lon", [(i, (i + 1) % count) for i in range(count)])
    right = lax.ppermute(both[:, :HALO], "lon", [((i + 1) % count, i) for i in range(count)])
    wide = cells + 2 * HALO
    vmem = pl.BlockSpec(memory_space=pltpu.VMEM)

    def run(*refs):
        kernel(cells, tiles, *refs)

    return pl.pallas_call(
        run,
        out_shape=jax.ShapeDtypeStruct((1, *start.shape), jnp.float32),
        in_specs=[vmem] * 5,
        out_specs=vmem,
        scratch_shapes=[pltpu.VMEM((tiles, wide, LANES), jnp.float32)] * 27,
        compiler_params=pltpu.CompilerParams(vmem_limit_bytes=VMEM_LIMIT),
        name="parareal",
    )(start, depth, left, right, jnp.asarray(table))


def solution(mesh):
    return jax.shard_map(
        body,
        mesh=mesh,
        in_specs=(P(None, "lon", None), P("lon", None)),
        out_specs=P("tm", None, "lon", None),
        check_vma=False,
    )
```

```python
import math

import jax
import jax.numpy as jnp
import numpy as np
from jax import lax
from jax.experimental import pallas as pl
from jax.experimental.pallas import tpu as pltpu
from jax.sharding import PartitionSpec as P

STEPS = 3
ROUNDS = 2
LAT_LIMIT = 1.2
COURANT = 1.2
DEPTH_MAX = 1.5
GRAVITY = 1.0
TURN_RATE = 0.15

HALO = 2 * STEPS * ROUNDS
ROWS = 8
LANES = 128
VMEM_LIMIT = 16 << 20

EAST, POLE, DIVERGE, SPIN_U, SPIN_V, GRAD_E, GRAD_N, TURN_C, TURN_U, TURN_V, EAST_INV, POLE_INV = range(12)


def lat_table(lon_cells, lat_cells):
    latitude = -LAT_LIMIT + (np.arange(lat_cells) + 0.5) * (2.0 * LAT_LIMIT / lat_cells)
    cosine = np.cos(latitude)
    north_spacing = 2.0 * LAT_LIMIT / lat_cells
    east_spacing = cosine * (2.0 * math.pi / lon_cells)
    narrowest = math.cos(LAT_LIMIT - LAT_LIMIT / lat_cells) * 2.0 * math.pi / lon_cells
    time_step = COURANT / (
        math.sqrt(DEPTH_MAX * GRAVITY) * math.sqrt(1.0 / narrowest**2 + 1.0 / north_spacing**2)
    )
    spin = TURN_RATE * np.sin(latitude)
    turning = spin * STEPS
    east = time_step / (2.0 * east_spacing)
    north = time_step / (2.0 * north_spacing)
    rows = [None] * 12
    rows[EAST] = east
    rows[POLE] = cosine
    rows[DIVERGE] = north / cosine
    rows[SPIN_U] = spin * east / cosine
    rows[SPIN_V] = spin * cosine / east
    rows[GRAD_E] = GRAVITY * east
    rows[GRAD_N] = GRAVITY * north + 0.0 * cosine
    rows[TURN_C] = np.cos(turning)
    rows[TURN_U] = np.sin(turning) * east / cosine
    rows[TURN_V] = np.sin(turning) * cosine / east
    rows[EAST_INV] = 1.0 / east
    rows[POLE_INV] = 1.0 / cosine
    table = np.stack(rows).astype(np.float32)
    table = table.reshape(12, LANES, lat_cells // LANES).swapaxes(1, 2).reshape(12, 1, lat_cells)
    return np.broadcast_to(table, (12, ROWS, lat_cells)).copy()


def windows(low, high):
    starts = list(range(low, high - ROWS + 1, ROWS))
    if starts[-1] + ROWS < high:
        starts.append(high - ROWS)
    return starts


def deal(tiles):
    lat = np.arange(tiles * LANES)
    matrix = np.zeros((lat.size, lat.size), np.float32)
    matrix[lat, (lat % tiles) * LANES + lat // tiles] = 1.0
    return matrix


def times_one_hot(values, matrix):
    pieces = []
    rest = values
    for _ in range(3):
        pieces.append(rest.astype(jnp.bfloat16))
        rest = rest - pieces[-1].astype(jnp.float32)
    count = values.shape[0]
    out = jnp.dot(jnp.concatenate(pieces, axis=0), matrix, preferred_element_type=jnp.float32)
    return out[:count] + out[count : 2 * count] + out[2 * count :]


def lanes(t):
    return slice(t * LANES, (t + 1) * LANES)


def put_fields(dealt, table, tiles, count, first_row, step, refs, base):
    for t in range(tiles):
        h, u, v, d = (
            dealt[first_row + f * step : first_row + f * step + count, lanes(t)] for f in range(4)
        )
        he = d * table[EAST, :1, lanes(t)]
        hp = d * table[POLE, :1, lanes(t)]
        rows = slice(base, base + count)
        values = (h, u * he, v * hp, he * table[GRAD_E, :1, lanes(t)], hp * table[GRAD_N, :1, lanes(t)])
        for ref, value in zip(refs, values):
            ref[t, rows, :] = value


def prepare(cells, tiles, start, depth, table, dealing, out):
    own = jnp.concatenate([start[0], start[1], start[2], depth[...]], axis=0)
    dealt = times_one_hot(own, dealing[...])
    put_fields(dealt, table, tiles, cells, 0, cells, [out.at[k] for k in range(5)], 0)
    for t in range(tiles):
        over = 1.0 / dealt[3 * cells :, lanes(t)]
        out[5, t] = over * table[EAST_INV, :1, lanes(t)]
        out[6, t] = over * table[POLE_INV, :1, lanes(t)]


def kernel(cells, tiles, own, left, right, table, dealing, undealing, ends, *scratch):
    (s_h, u_a, u_b, v_h, v_a, v_b, w_h, w_a, w_b, grad_e, grad_n) = scratch[:11]
    temps1 = scratch[11:17]
    temps2 = scratch[17:23]
    wide = cells + 2 * HALO
    reach = 2 * STEPS
    number = lax.axis_index("tm")
    lane = lax.broadcasted_iota(jnp.int32, (ROWS, LANES), 1)
    first = lane == 0
    last = lane == LANES - 1

    def const(row, t):
        return table[row, :, t * LANES : (t + 1) * LANES]

    def at(ref, t, row):
        return ref[t, row : row + ROWS, :]

    def put(ref, t, row, value):
        ref[t, row : row + ROWS, :] = value

    def north_diff(parts):
        above = parts[1:] + [jnp.where(last, 0.0, pltpu.roll(parts[0], LANES - 1, 1))]
        below = [jnp.where(first, 0.0, pltpu.roll(parts[-1], 1, 1))] + parts[:-1]
        return [up - down for up, down in zip(above, below)]

    def consts(*rows):
        return [[const(row, t) for t in range(tiles)] for row in rows]

    fields = (s_h, u_a, u_b, grad_e, grad_n)
    dealt = times_one_hot(jnp.concatenate([left[...], right[...]], axis=0), dealing[...])
    put_fields(dealt, table, tiles, HALO, 0, HALO, fields, 0)
    put_fields(dealt, table, tiles, HALO, 4 * HALO, HALO, fields, HALO + cells)
    for k, ref in enumerate(fields):
        ref[:, HALO : HALO + cells, :] = own[k]

    def fine(source, low, high, temps, finish):
        state = source
        for step in range(STEPS):
            height, alpha, beta = state
            new_h, new_a, new_b = temps[3 * (step % 2) : 3 * (step % 2) + 3]
            (diverge,) = consts(DIVERGE)
            for row in windows(low + 1, high - 1):
                flux = north_diff([at(beta, t, row) for t in range(tiles)])
                for t in range(tiles):
                    value = at(height, t, row) - (at(alpha, t, row + 1) - at(alpha, t, row - 1))
                    put(new_h, t, row, value - diverge[t] * flux[t])
            low, high = low + 2, high - 2
            rows = windows(low, high)
            if step == STEPS - 1:
                rows = list(range(low, high, ROWS))
            spin_u, spin_v = consts(SPIN_U, SPIN_V)
            for row in rows:
                here = [at(new_h, t, row) for t in range(tiles)]
                slope = north_diff(here)
                for t in range(tiles):
                    b = at(beta, t, row)
                    east = at(new_h, t, row + 1) - at(new_h, t, row - 1)
                    a = at(alpha, t, row) + spin_u[t] * b - at(grad_e, t, row) * east
                    b = b - spin_v[t] * a - at(grad_n, t, row) * slope[t]
                    if step == STEPS - 1:
                        finish(t, row, here[t], a, b)
                    else:
                        put(new_a, t, row, a)
                        put(new_b, t, row, b)
            state = (new_h, new_a, new_b)

    def turn(a, b, t):
        c = const(TURN_C, t)
        return c * a + const(TURN_U, t) * b, c * b - const(TURN_V, t) * a

    def first_slice():
        def finish(t, row, h, a, b):
            for ref, value in zip((v_h, v_a, v_b), (h, a, b)):
                put(ref, t, row, value)
            for ref, value in zip((w_h, w_a, w_b), (h, a, b)):
                put(ref, t, row, value)

        fine((s_h, u_a, u_b), 0, wide, temps1, finish)

    def round_one():
        def finish(t, row, h, a, b):
            put(v_h, t, row, h + (at(v_h, t, row) - at(s_h, t, row)))
            da, db = turn(
                at(v_a, t, row) - at(u_a, t, row), at(v_b, t, row) - at(u_b, t, row), t
            )
            put(v_a, t, row, a + da)
            put(v_b, t, row, b + db)

        fine((s_h, u_a, u_b), 0, wide, temps1, finish)

    def turn_guess():
        for row in range(0, wide, ROWS):
            for t in range(tiles):
                a, b = turn(at(u_a, t, row), at(u_b, t, row), t)
                put(u_a, t, row, a)
                put(u_b, t, row, b)

    def round_two():
        def finish(t, row, h, a, b):
            da, db = turn(
                at(w_a, t, row) - at(v_a, t, row), at(w_b, t, row) - at(v_b, t, row), t
            )
            put(w_h, t, row, h + (at(w_h, t, row) - at(v_h, t, row)))
            put(w_a, t, row, a + da)
            put(w_b, t, row, b + db)

        fine((v_h, v_a, v_b), reach, wide - reach, temps2, finish)

    @pl.when(number == 0)
    def _():
        for source, targets in zip((s_h, u_a, u_b), ((v_h, w_h), (v_a, w_a), (v_b, w_b))):
            for target in targets:
                target[...] = source[...]

    pl.when(number > 0)(first_slice)

    def both(index, carry):
        turn_guess()
        round_two()
        round_one()
        return carry

    lax.fori_loop(1, number, both, 0)
    round_two()
    rows = slice(HALO, HALO + cells)
    whole = [
        jnp.concatenate([w_h[t, rows, :] for t in range(tiles)], axis=1),
        jnp.concatenate([w_a[t, rows, :] * own[5, t] for t in range(tiles)], axis=1),
        jnp.concatenate([w_b[t, rows, :] * own[6, t] for t in range(tiles)], axis=1),
    ]
    whole = times_one_hot(jnp.concatenate(whole, axis=0), undealing[...])
    for field in range(3):
        ends[0, field] = whole[field * cells : (field + 1) * cells]


def body(start, depth):
    count = lax.axis_size("lon")
    _, cells, lat_cells = start.shape
    tiles = lat_cells // LANES
    table = lat_table(cells * count, lat_cells)
    dealing = deal(tiles)

    def edge(low, high):
        return jnp.concatenate([start[:, low:high], depth[None, low:high]], axis=0).reshape(-1, lat_cells)

    ring = [(i, (i + 1) % count) for i in range(count)]
    left = lax.ppermute(edge(cells - HALO, cells), "lon", ring)
    right = lax.ppermute(edge(0, HALO), "lon", [(j, i) for i, j in ring])
    wide = cells + 2 * HALO
    vmem = pl.BlockSpec(memory_space=pltpu.VMEM)
    params = pltpu.CompilerParams(vmem_limit_bytes=VMEM_LIMIT)
    table = jnp.asarray(table)
    undealing = jnp.asarray(dealing.T, jnp.bfloat16)
    dealing = jnp.asarray(dealing, jnp.bfloat16)

    own = pl.pallas_call(
        lambda *refs: prepare(cells, tiles, *refs),
        out_shape=jax.ShapeDtypeStruct((7, tiles, cells, LANES), jnp.float32),
        in_specs=[vmem] * 4,
        out_specs=vmem,
        compiler_params=params,
        cost_estimate=pl.CostEstimate(flops=10**9, bytes_accessed=10**7, transcendentals=0),
        name="prepare",
    )(start, depth, table, dealing)
    return pl.pallas_call(
        lambda *refs: kernel(cells, tiles, *refs),
        out_shape=jax.ShapeDtypeStruct((1, *start.shape), jnp.float32),
        in_specs=[vmem] * 6,
        out_specs=vmem,
        scratch_shapes=[pltpu.VMEM((tiles, wide, LANES), jnp.float32)] * 23,
        compiler_params=params,
        name="parareal",
    )(own, left, right, table, dealing, undealing)


def solution(mesh):
    return jax.shard_map(
        body,
        mesh=mesh,
        in_specs=(P(None, "lon", None), P("lon", None)),
        out_specs=P("tm", None, "lon", None),
        check_vma=False,
    )
```

```python
import math

import jax
import jax.numpy as jnp
import numpy as np
from jax import lax
from jax.experimental import pallas as pl
from jax.experimental.pallas import tpu as pltpu
from jax.sharding import PartitionSpec as P

STEPS = 3
ROUNDS = 2
LAT_LIMIT = 1.2
COURANT = 1.2
DEPTH_MAX = 1.5
GRAVITY = 1.0
TURN_RATE = 0.15

HALO = 2 * STEPS * ROUNDS
ROWS = 8
LANES = 128
VMEM_LIMIT = 16 << 20

EAST, POLE, DIVERGE, SPIN_U, SPIN_V, GRAD_E, GRAD_N, TURN_C, TURN_U, TURN_V, EAST_INV, POLE_INV = range(12)


def lat_table(lon_cells, lat_cells):
    latitude = -LAT_LIMIT + (np.arange(lat_cells) + 0.5) * (2.0 * LAT_LIMIT / lat_cells)
    cosine = np.cos(latitude)
    north_spacing = 2.0 * LAT_LIMIT / lat_cells
    east_spacing = cosine * (2.0 * math.pi / lon_cells)
    narrowest = math.cos(LAT_LIMIT - LAT_LIMIT / lat_cells) * 2.0 * math.pi / lon_cells
    time_step = COURANT / (
        math.sqrt(DEPTH_MAX * GRAVITY) * math.sqrt(1.0 / narrowest**2 + 1.0 / north_spacing**2)
    )
    spin = TURN_RATE * np.sin(latitude)
    turning = spin * STEPS
    east = time_step / (2.0 * east_spacing)
    north = time_step / (2.0 * north_spacing)
    rows = [None] * 12
    rows[EAST] = east
    rows[POLE] = cosine
    rows[DIVERGE] = north / cosine
    rows[SPIN_U] = spin * east / cosine
    rows[SPIN_V] = spin * cosine / east
    rows[GRAD_E] = GRAVITY * east
    rows[GRAD_N] = GRAVITY * north + 0.0 * cosine
    rows[TURN_C] = np.cos(turning)
    rows[TURN_U] = np.sin(turning) * east / cosine
    rows[TURN_V] = np.sin(turning) * cosine / east
    rows[EAST_INV] = 1.0 / east
    rows[POLE_INV] = 1.0 / cosine
    table = np.stack(rows).astype(np.float32)
    return table.reshape(12, LANES, lat_cells // LANES).swapaxes(1, 2).reshape(12, lat_cells)


def windows(low, high):
    starts = list(range(low, high - ROWS + 1, ROWS))
    if starts[-1] + ROWS < high:
        starts.append(high - ROWS)
    return starts


def deal(tiles, dealing, undealing):
    lat_cells = tiles * LANES
    for t in range(tiles):
        lat = lax.broadcasted_iota(jnp.int32, (lat_cells, LANES), 0)
        lane = lax.broadcasted_iota(jnp.int32, (lat_cells, LANES), 1)
        hit = lat == lane * tiles + t
        dealing[:, lanes(t)] = jnp.where(hit, 1.0, 0.0).astype(jnp.bfloat16)
        lat = lax.broadcasted_iota(jnp.int32, (LANES, lat_cells), 1)
        lane = lax.broadcasted_iota(jnp.int32, (LANES, lat_cells), 0)
        hit = lat == lane * tiles + t
        undealing[lanes(t), :] = jnp.where(hit, 1.0, 0.0).astype(jnp.bfloat16)


def times_one_hot(values, matrix):
    pieces = []
    rest = values
    for _ in range(3):
        pieces.append(rest.astype(jnp.bfloat16))
        rest = rest - pieces[-1].astype(jnp.float32)
    count = values.shape[0]
    out = jnp.dot(jnp.concatenate(pieces, axis=0), matrix, preferred_element_type=jnp.float32)
    return out[:count] + out[count : 2 * count] + out[2 * count :]


def lanes(t):
    return slice(t * LANES, (t + 1) * LANES)


def put_fields(dealt, table, tiles, count, first_row, step, refs, base):
    for t in range(tiles):
        h, u, v, d = (
            dealt[first_row + f * step : first_row + f * step + count, lanes(t)] for f in range(4)
        )
        he = d * table[EAST, :1, lanes(t)]
        hp = d * table[POLE, :1, lanes(t)]
        rows = slice(base, base + count)
        values = (h, u * he, v * hp, he * table[GRAD_E, :1, lanes(t)], hp * table[GRAD_N, :1, lanes(t)])
        for ref, value in zip(refs, values):
            ref[t, rows, :] = value


def prepare(cells, tiles, start, depth, rows, out, table, dealing, undealing):
    for row in range(rows.shape[0]):
        table[row] = jnp.broadcast_to(rows[row : row + 1, :], (ROWS, tiles * LANES))
    deal(tiles, dealing, undealing)
    own = jnp.concatenate([start[0], start[1], start[2], depth[...]], axis=0)
    dealt = times_one_hot(own, dealing[...])
    put_fields(dealt, table, tiles, cells, 0, cells, [out.at[k] for k in range(5)], 0)
    for t in range(tiles):
        over = 1.0 / dealt[3 * cells :, lanes(t)]
        out[5, t] = over * table[EAST_INV, :1, lanes(t)]
        out[6, t] = over * table[POLE_INV, :1, lanes(t)]


def kernel(cells, tiles, own, left, right, table, dealing, undealing, ends, *scratch):
    (s_h, u_a, u_b, v_h, v_a, v_b, w_h, w_a, w_b, grad_e, grad_n) = scratch[:11]
    temps1 = scratch[11:17]
    temps2 = scratch[17:23]
    wide = cells + 2 * HALO
    reach = 2 * STEPS
    number = lax.axis_index("tm")
    lane = lax.broadcasted_iota(jnp.int32, (ROWS, LANES), 1)
    first = lane == 0
    last = lane == LANES - 1

    def const(row, t):
        return table[row, :, t * LANES : (t + 1) * LANES]

    def at(ref, t, row):
        return ref[t, row : row + ROWS, :]

    def put(ref, t, row, value):
        ref[t, row : row + ROWS, :] = value

    def north_diff(parts):
        above = parts[1:] + [jnp.where(last, 0.0, pltpu.roll(parts[0], LANES - 1, 1))]
        below = [jnp.where(first, 0.0, pltpu.roll(parts[-1], 1, 1))] + parts[:-1]
        return [up - down for up, down in zip(above, below)]

    def consts(*rows):
        return [[const(row, t) for t in range(tiles)] for row in rows]

    fields = (s_h, u_a, u_b, grad_e, grad_n)
    flat = scratch[23]
    for side, halo in enumerate((left, right)):
        for field in range(4):
            first_row = (4 * side + field) * HALO
            flat[first_row : first_row + HALO, :] = halo[field]
    dealt = times_one_hot(flat[...], dealing[...])
    put_fields(dealt, table, tiles, HALO, 0, HALO, fields, 0)
    put_fields(dealt, table, tiles, HALO, 4 * HALO, HALO, fields, HALO + cells)
    for k, ref in enumerate(fields):
        ref[:, HALO : HALO + cells, :] = own[k]

    def fine(source, low, high, temps, finish):
        state = source
        for step in range(STEPS):
            height, alpha, beta = state
            new_h, new_a, new_b = temps[3 * (step % 2) : 3 * (step % 2) + 3]
            (diverge,) = consts(DIVERGE)
            for row in windows(low + 1, high - 1):
                flux = north_diff([at(beta, t, row) for t in range(tiles)])
                for t in range(tiles):
                    value = at(height, t, row) - (at(alpha, t, row + 1) - at(alpha, t, row - 1))
                    put(new_h, t, row, value - diverge[t] * flux[t])
            low, high = low + 2, high - 2
            rows = windows(low, high)
            if step == STEPS - 1:
                rows = list(range(low, high, ROWS))
            spin_u, spin_v = consts(SPIN_U, SPIN_V)
            for row in rows:
                here = [at(new_h, t, row) for t in range(tiles)]
                slope = north_diff(here)
                for t in range(tiles):
                    b = at(beta, t, row)
                    east = at(new_h, t, row + 1) - at(new_h, t, row - 1)
                    a = at(alpha, t, row) + spin_u[t] * b - at(grad_e, t, row) * east
                    b = b - spin_v[t] * a - at(grad_n, t, row) * slope[t]
                    if step == STEPS - 1:
                        finish(t, row, here[t], a, b)
                    else:
                        put(new_a, t, row, a)
                        put(new_b, t, row, b)
            state = (new_h, new_a, new_b)

    def turn(a, b, t):
        c = const(TURN_C, t)
        return c * a + const(TURN_U, t) * b, c * b - const(TURN_V, t) * a

    def first_slice():
        def finish(t, row, h, a, b):
            for ref, value in zip((v_h, v_a, v_b), (h, a, b)):
                put(ref, t, row, value)
            for ref, value in zip((w_h, w_a, w_b), (h, a, b)):
                put(ref, t, row, value)

        fine((s_h, u_a, u_b), 0, wide, temps1, finish)

    def round_one():
        def finish(t, row, h, a, b):
            put(v_h, t, row, h + (at(v_h, t, row) - at(s_h, t, row)))
            da, db = turn(
                at(v_a, t, row) - at(u_a, t, row), at(v_b, t, row) - at(u_b, t, row), t
            )
            put(v_a, t, row, a + da)
            put(v_b, t, row, b + db)

        fine((s_h, u_a, u_b), 0, wide, temps1, finish)

    def turn_guess():
        for row in range(0, wide, ROWS):
            for t in range(tiles):
                a, b = turn(at(u_a, t, row), at(u_b, t, row), t)
                put(u_a, t, row, a)
                put(u_b, t, row, b)

    def round_two():
        def finish(t, row, h, a, b):
            da, db = turn(
                at(w_a, t, row) - at(v_a, t, row), at(w_b, t, row) - at(v_b, t, row), t
            )
            put(w_h, t, row, h + (at(w_h, t, row) - at(v_h, t, row)))
            put(w_a, t, row, a + da)
            put(w_b, t, row, b + db)

        fine((v_h, v_a, v_b), reach, wide - reach, temps2, finish)

    @pl.when(number == 0)
    def _():
        for source, targets in zip((s_h, u_a, u_b), ((v_h, w_h), (v_a, w_a), (v_b, w_b))):
            for target in targets:
                target[...] = source[...]

    pl.when(number > 0)(first_slice)

    def both(index, carry):
        turn_guess()
        round_two()
        round_one()
        return carry

    lax.fori_loop(1, number, both, 0)
    round_two()
    rows = slice(HALO, HALO + cells)
    whole = [
        jnp.concatenate([w_h[t, rows, :] for t in range(tiles)], axis=1),
        jnp.concatenate([w_a[t, rows, :] * own[5, t] for t in range(tiles)], axis=1),
        jnp.concatenate([w_b[t, rows, :] * own[6, t] for t in range(tiles)], axis=1),
    ]
    whole = times_one_hot(jnp.concatenate(whole, axis=0), undealing[...])
    for field in range(3):
        ends[0, field] = whole[field * cells : (field + 1) * cells]


def body(start, depth):
    count = lax.axis_size("lon")
    _, cells, lat_cells = start.shape
    tiles = lat_cells // LANES
    table = jnp.asarray(lat_table(cells * count, lat_cells))
    both = jnp.concatenate([start, depth[None]], axis=0)
    ring = [(i, (i + 1) % count) for i in range(count)]
    left = lax.ppermute(both[:, cells - HALO :], "lon", ring)
    right = lax.ppermute(both[:, :HALO], "lon", [(j, i) for i, j in ring])
    wide = cells + 2 * HALO
    vmem = pl.BlockSpec(memory_space=pltpu.VMEM)
    params = pltpu.CompilerParams(
        vmem_limit_bytes=VMEM_LIMIT
    )
    prepared = pl.pallas_call(
        lambda *refs: prepare(cells, tiles, *refs),
        out_shape=(
            jax.ShapeDtypeStruct((7, tiles, cells, LANES), jnp.float32),
            jax.ShapeDtypeStruct((table.shape[0], ROWS, lat_cells), jnp.float32),
            jax.ShapeDtypeStruct((lat_cells, lat_cells), jnp.bfloat16),
            jax.ShapeDtypeStruct((lat_cells, lat_cells), jnp.bfloat16),
        ),
        in_specs=[vmem] * 3,
        out_specs=[vmem] * 4,
        compiler_params=params,
        cost_estimate=pl.CostEstimate(flops=10**9, bytes_accessed=10**7, transcendentals=0),
        name="prepare",
    )(start, depth, table)
    return pl.pallas_call(
        lambda *refs: kernel(cells, tiles, *refs),
        out_shape=jax.ShapeDtypeStruct((1, *start.shape), jnp.float32),
        in_specs=[vmem] * 6,
        out_specs=vmem,
        scratch_shapes=[pltpu.VMEM((tiles, wide, LANES), jnp.float32)] * 23
        + [pltpu.VMEM((8 * HALO, lat_cells), jnp.float32)],
        compiler_params=params,
        name="parareal",
    )(prepared[0], left, right, *prepared[1:])


def solution(mesh):
    return jax.shard_map(
        body,
        mesh=mesh,
        in_specs=(P(None, "lon", None), P("lon", None)),
        out_specs=P("tm", None, "lon", None),
        check_vma=False,
    )
```

```python
import math

import jax
import jax.numpy as jnp
import numpy as np
from jax import lax
from jax.experimental import pallas as pl
from jax.experimental.pallas import tpu as pltpu
from jax.sharding import PartitionSpec as P

STEPS = 3
ROUNDS = 2
LAT_LIMIT = 1.2
COURANT = 1.2
DEPTH_MAX = 1.5
GRAVITY = 1.0
TURN_RATE = 0.15

HALO = 2 * STEPS * ROUNDS
ROWS = 8
LANES = 128
DEAL_ROWS = 64
FIRST, MORE = 3, 4
VMEM_LIMIT = 24 << 20

EAST, POLE, DIVERGE, SPIN_U, SPIN_V, GRAD_E, GRAD_N, TURN_C, TURN_U, TURN_V, EAST_INV, POLE_INV = range(12)


def lat_table(lon_cells, lat_cells):
    latitude = -LAT_LIMIT + (np.arange(lat_cells) + 0.5) * (2.0 * LAT_LIMIT / lat_cells)
    cosine = np.cos(latitude)
    north_spacing = 2.0 * LAT_LIMIT / lat_cells
    east_spacing = cosine * (2.0 * math.pi / lon_cells)
    narrowest = math.cos(LAT_LIMIT - LAT_LIMIT / lat_cells) * 2.0 * math.pi / lon_cells
    time_step = COURANT / (
        math.sqrt(DEPTH_MAX * GRAVITY) * math.sqrt(1.0 / narrowest**2 + 1.0 / north_spacing**2)
    )
    spin = TURN_RATE * np.sin(latitude)
    turning = spin * STEPS
    east = time_step / (2.0 * east_spacing)
    north = time_step / (2.0 * north_spacing)
    rows = [None] * 12
    rows[EAST] = east
    rows[POLE] = cosine
    rows[DIVERGE] = north / cosine
    rows[SPIN_U] = spin * east / cosine
    rows[SPIN_V] = spin * cosine / east
    rows[GRAD_E] = GRAVITY * east
    rows[GRAD_N] = GRAVITY * north + 0.0 * cosine
    rows[TURN_C] = np.cos(turning)
    rows[TURN_U] = np.sin(turning) * east / cosine
    rows[TURN_V] = np.sin(turning) * cosine / east
    rows[EAST_INV] = 1.0 / east
    rows[POLE_INV] = 1.0 / cosine
    table = np.stack(rows).astype(np.float32)
    return table.reshape(12, LANES, lat_cells // LANES).swapaxes(1, 2).reshape(12, lat_cells)


def windows(low, high):
    starts = list(range(low, high - ROWS + 1, ROWS))
    if starts[-1] + ROWS < high:
        starts.append(high - ROWS)
    return starts


def deal(tiles, dealing, undealing):
    def block(index, carry):
        start = pl.multiple_of(index * DEAL_ROWS, DEAL_ROWS)
        row = start + lax.broadcasted_iota(jnp.int32, (DEAL_ROWS, LANES), 0)
        lane = lax.broadcasted_iota(jnp.int32, (DEAL_ROWS, LANES), 1)
        place = row % LANES * tiles + row // LANES
        for t in range(tiles):
            hit = row == lane * tiles + t
            dealing[pl.ds(start, DEAL_ROWS), lanes(t)] = jnp.where(hit, 1.0, 0.0).astype(jnp.bfloat16)
            hit = place == lane + t * LANES
            undealing[pl.ds(start, DEAL_ROWS), lanes(t)] = jnp.where(hit, 1.0, 0.0).astype(jnp.bfloat16)
        return carry

    lax.fori_loop(0, tiles * LANES // DEAL_ROWS, block, 0)


def times_one_hot(values, matrix):
    pieces = []
    rest = values
    for _ in range(3):
        pieces.append(rest.astype(jnp.bfloat16))
        rest = rest - pieces[-1].astype(jnp.float32)
    count = values.shape[0]
    out = jnp.dot(jnp.concatenate(pieces, axis=0), matrix, preferred_element_type=jnp.float32)
    return out[:count] + out[count : 2 * count] + out[2 * count :]


def lanes(t):
    return slice(t * LANES, (t + 1) * LANES)


def put_fields(dealt, table, tiles, count, first_row, step, refs, base):
    for t in range(tiles):
        h, u, v, d = (
            dealt[first_row + f * step : first_row + f * step + count, lanes(t)] for f in range(4)
        )
        he = d * table[EAST, :1, lanes(t)]
        hp = d * table[POLE, :1, lanes(t)]
        rows = slice(base, base + count)
        values = (h, u * he, v * hp, he * table[GRAD_E, :1, lanes(t)], hp * table[GRAD_N, :1, lanes(t)])
        for ref, value in zip(refs, values):
            ref[t, rows, :] = value


def windows(low, high):
    starts = list(range(low, high - ROWS + 1, ROWS))
    if starts[-1] + ROWS < high:
        starts.append(high - ROWS)
    return starts


def shrinking(low, high):
    return [
        (windows(low + 2 * s - 1, high - 2 * s + 1), windows(low + 2 * s, high - 2 * s))
        for s in range(1, STEPS + 1)
    ]


def strips(wide):
    offsets = range(0, HALO, ROWS)
    return [
        (
            [2 * s - 1 + k for k in offsets] + [wide - 2 * s + 1 - ROWS - k for k in offsets],
            [2 * s + k for k in offsets] + [wide - 2 * s - ROWS - k for k in offsets],
        )
        for s in range(1, STEPS + 1)
    ]


def joints(low, high):
    return [(low + 2 * s + 3, high - 2 * s - 3 - ROWS) for s in range(1, STEPS)]


def at(ref, t, row):
    return ref[t, row : row + ROWS, :]


def put(ref, t, row, value):
    ref[t, row : row + ROWS, :] = value


class Fluid:
    def __init__(self, table, tiles, grad_e, grad_n):
        lane = lax.broadcasted_iota(jnp.int32, (ROWS, LANES), 1)
        self.first, self.last = lane == 0, lane == LANES - 1
        self.table, self.tiles = table, tiles
        self.grad_e, self.grad_n = grad_e, grad_n

    def const(self, row, t):
        return self.table[row, :, lanes(t)]

    def consts(self, *rows):
        return [[self.const(row, t) for t in range(self.tiles)] for row in rows]

    def north_diff(self, parts):
        wrapped = pltpu.roll(parts[0], LANES - 1, 1)
        above = parts[1:] + [jnp.where(self.last, 0.0, wrapped)]
        wrapped = pltpu.roll(parts[-1], 1, 1)
        below = [jnp.where(self.first, 0.0, wrapped)] + parts[:-1]
        return [up - down for up, down in zip(above, below)]

    def turn(self, a, b, t):
        c = self.const(TURN_C, t)
        return c * a + self.const(TURN_U, t) * b, c * b - self.const(TURN_V, t) * a

    def fine(self, state, temps, plan, finish):
        tiles = range(self.tiles)
        for step, (height_rows, rest_rows) in enumerate(plan):
            height, alpha, beta = state
            new_h, new_a, new_b = temps[step]
            (diverge,) = self.consts(DIVERGE)
            for row in height_rows:
                flux = self.north_diff([at(beta, t, row) for t in tiles])
                for t in tiles:
                    value = at(height, t, row) - (at(alpha, t, row + 1) - at(alpha, t, row - 1))
                    put(new_h, t, row, value - diverge[t] * flux[t])
            spin_u, spin_v = self.consts(SPIN_U, SPIN_V)
            for row in rest_rows:
                here = [at(new_h, t, row) for t in tiles]
                slope = self.north_diff(here)
                for t in tiles:
                    b = at(beta, t, row)
                    east = at(new_h, t, row + 1) - at(new_h, t, row - 1)
                    a = at(alpha, t, row) + spin_u[t] * b - at(self.grad_e, t, row) * east
                    b = b - spin_v[t] * a - at(self.grad_n, t, row) * slope[t]
                    if step == STEPS - 1:
                        finish(t, row, here[t], a, b)
                    else:
                        put(new_a, t, row, a)
                        put(new_b, t, row, b)
            state = (new_h, new_a, new_b)

    def turn_rows(self, source, target, rows):
        for row in rows:
            for t in range(self.tiles):
                a, b = self.turn(at(source[0], t, row), at(source[1], t, row), t)
                put(target[0], t, row, a)
                put(target[1], t, row, b)


def stages(refs):
    return [refs[0:3], refs[3:6], (refs[6], None, None)]


def streams_of(refs):
    return [stages(refs[7 * k : 7 * k + 7]) for k in range(len(refs) // 7)]


def in_blocks(number, one_block):
    one_block(0, FIRST)

    def more(index, carry):
        one_block(FIRST + MORE * index, MORE)
        return carry

    lax.fori_loop(0, (number + MORE - FIRST - 1) // MORE, more, 0)


def prepare(cells, tiles, stacked, out, table, dealing, undealing, inner, joint, *scratch):
    number = lax.axis_index("tm")
    for row in range(table.shape[0]):
        source = stacked[4 * cells + row : 4 * cells + row + 1, :]
        table[row] = jnp.broadcast_to(source, (ROWS, tiles * LANES))
    deal(tiles, dealing, undealing)
    dealt = times_one_hot(stacked[: 4 * cells, :], dealing[...])
    put_fields(dealt, table, tiles, cells, 0, cells, [out.at[k] for k in range(5)], 0)
    for t in range(tiles):
        over = 1.0 / dealt[3 * cells :, lanes(t)]
        out[5, t] = over * table[EAST_INV, :1, lanes(t)]
        out[6, t] = over * table[POLE_INV, :1, lanes(t)]

    fluid = Fluid(table, tiles, out.at[3], out.at[4])
    reach = 2 * STEPS
    plan = shrinking(0, cells)
    guesses = [scratch[2 * k : 2 * k + 2] for k in range(MORE)]
    temps_of = streams_of(scratch[2 * MORE :])
    guesses[0][0][...] = out[1]
    guesses[0][1][...] = out[2]
    for field in range(3):
        inner[0, field, :, : cells - 2 * reach, :] = out[field, :, reach : cells - reach, :]
    every = range(0, cells, ROWS)

    def one_block(start, count):
        for k in range(count):
            one_slice(start + k, guesses[k], temps_of[k])
            fluid.turn_rows(guesses[k], guesses[(k + 1) % count], every)

    def one_slice(m, guess, temps):
        before = [inner.at[m, field] for field in range(3)]
        after = [inner.at[m + 1, field] for field in range(3)]

        def finish(t, row, h, a, b):
            own_row = row - reach
            put(after[0], t, own_row, h + (at(before[0], t, own_row) - out[0, t, row : row + ROWS, :]))
            da, db = fluid.turn(
                at(before[1], t, own_row) - at(guess[0], t, row),
                at(before[2], t, own_row) - at(guess[1], t, row),
                t,
            )
            put(after[1], t, own_row, a + da)
            put(after[2], t, own_row, b + db)

        fluid.fine((out.at[0], *guess), temps, plan, finish)
        for step, sides in enumerate(joints(0, cells)):
            for side, row in enumerate(sides):
                for field in range(3):
                    for t in range(tiles):
                        joint[m, step, side, field, t] = at(temps[step][field], t, row)

    in_blocks(number, one_block)


def kernel(cells, tiles, own, left, right, table, dealing, undealing, inner, joint, ends, *scratch):
    (s_h, grad_e, grad_n, w_h, w_a, w_b, firsts, flat) = scratch[:8]
    guesses = [scratch[8 + 2 * k : 10 + 2 * k] for k in range(MORE)]
    temps_of = streams_of(scratch[8 + 2 * MORE :])
    wide = cells + 2 * HALO
    reach = 2 * STEPS
    number = lax.axis_index("tm")
    fluid = Fluid(table, tiles, grad_e, grad_n)

    fields = (s_h, *guesses[0], grad_e, grad_n)
    for side, halo in enumerate((left, right)):
        for field in range(4):
            first_row = (4 * side + field) * HALO
            flat[first_row : first_row + HALO, :] = halo[field]
    dealt = times_one_hot(flat[...], dealing[...])
    put_fields(dealt, table, tiles, HALO, 0, HALO, fields, 0)
    put_fields(dealt, table, tiles, HALO, 4 * HALO, HALO, fields, HALO + cells)
    for k, ref in enumerate(fields):
        ref[:, HALO : HALO + cells, :] = own[k]
    for field, ref in enumerate(fields[:3]):
        firsts[0, field] = ref[...]

    edge_rows = [*range(0, HALO + ROWS, ROWS)]
    edge_rows = sorted({*edge_rows, *(wide - ROWS - row for row in edge_rows)})

    def round_one(m, guess, temps):
        before = [firsts.at[m, field] for field in range(3)]
        after = [firsts.at[m + 1, field] for field in range(3)]

        def finish(t, row, h, a, b):
            put(after[0], t, row, h + (at(before[0], t, row) - at(s_h, t, row)))
            da, db = fluid.turn(
                at(before[1], t, row) - at(guess[0], t, row),
                at(before[2], t, row) - at(guess[1], t, row),
                t,
            )
            put(after[1], t, row, a + da)
            put(after[2], t, row, b + db)

        for step, sides in enumerate(joints(HALO, HALO + cells)):
            for side, row in enumerate(sides):
                for field in range(3):
                    for t in range(tiles):
                        put(temps[step][field], t, row, joint[m, step, side, field, t])
        fluid.fine((s_h, *guess), temps, strips(wide), finish)
        for row in windows(0, cells - 2 * reach):
            for field in range(3):
                for t in range(tiles):
                    put(after[field], t, HALO + reach + row, at(inner.at[m + 1, field], t, row))

    def block_one(start, count):
        for k in range(count):
            round_one(start + k, guesses[k], temps_of[k])
            fluid.turn_rows(guesses[k], guesses[(k + 1) % count], edge_rows)

    def round_two(m, temps):
        first = [firsts.at[m, field] for field in range(3)]
        active = m <= number

        def finish(t, row, h, a, b):
            wh, wa, wb = (at(ref, t, row) for ref in (w_h, w_a, w_b))
            da, db = fluid.turn(wa - at(first[1], t, row), wb - at(first[2], t, row), t)
            put(w_h, t, row, jnp.where(active, h + (wh - at(first[0], t, row)), wh))
            put(w_a, t, row, jnp.where(active, a + da, wa))
            put(w_b, t, row, jnp.where(active, b + db, wb))

        fluid.fine(first, temps, shrinking(reach, wide - reach), finish)

    def block_two(start, count):
        for k in range(count):
            round_two(1 + start + k, temps_of[k])

    in_blocks(number, block_one)
    for field, ref in enumerate((w_h, w_a, w_b)):
        ref[...] = firsts[1, field]

    @pl.when(number > 0)
    def _():
        in_blocks(number, block_two)

    rows = slice(HALO, HALO + cells)
    whole = [
        jnp.concatenate([w_h[t, rows, :] for t in range(tiles)], axis=1),
        jnp.concatenate([w_a[t, rows, :] * own[5, t] for t in range(tiles)], axis=1),
        jnp.concatenate([w_b[t, rows, :] * own[6, t] for t in range(tiles)], axis=1),
    ]
    whole = times_one_hot(jnp.concatenate(whole, axis=0), undealing[...])
    for field in range(3):
        ends[0, field] = whole[field * cells : (field + 1) * cells]


def body(start, depth):
    count = lax.axis_size("lon")
    _, cells, lat_cells = start.shape
    tiles = lat_cells // LANES
    slots = FIRST + MORE * (max(lax.axis_size("tm") - 1 - FIRST + MORE - 1, 0) // MORE)
    table = jnp.asarray(lat_table(cells * count, lat_cells))
    both = jnp.concatenate([start, depth[None]], axis=0)
    ring = [(i, (i + 1) % count) for i in range(count)]
    left = lax.ppermute(both[:, cells - HALO :], "lon", ring)
    right = lax.ppermute(both[:, :HALO], "lon", [(j, i) for i, j in ring])
    stacked = jnp.concatenate([start.reshape(-1, lat_cells), depth, table], axis=0)
    wide = cells + 2 * HALO
    inside = -(-(cells - 4 * STEPS) // ROWS) * ROWS
    vmem = pl.BlockSpec(memory_space=pltpu.VMEM)

    def shape(*dims, dtype=jnp.float32):
        return jax.ShapeDtypeStruct(dims, dtype)

    def scratch(*dims):
        return pltpu.VMEM(dims, jnp.float32)

    params = pltpu.CompilerParams(
        vmem_limit_bytes=VMEM_LIMIT
    )
    prepared = pl.pallas_call(
        lambda *refs: prepare(cells, tiles, *refs),
        out_shape=(
            shape(7, tiles, cells, LANES),
            shape(table.shape[0], ROWS, lat_cells),
            shape(lat_cells, lat_cells, dtype=jnp.bfloat16),
            shape(lat_cells, lat_cells, dtype=jnp.bfloat16),
            shape(slots + 1, 3, tiles, inside, LANES),
            shape(slots, STEPS - 1, 2, 3, tiles, ROWS, LANES),
        ),
        in_specs=[vmem],
        out_specs=[vmem] * 6,
        scratch_shapes=[scratch(tiles, cells, LANES)] * (9 * MORE),
        compiler_params=params,
        cost_estimate=pl.CostEstimate(flops=10**9, bytes_accessed=10**7, transcendentals=0),
        name="prepare",
    )(stacked)
    return pl.pallas_call(
        lambda *refs: kernel(cells, tiles, *refs),
        out_shape=shape(1, *start.shape),
        in_specs=[vmem] * 8,
        out_specs=vmem,
        scratch_shapes=[scratch(tiles, wide, LANES)] * 6
        + [scratch(slots + 1, 3, tiles, wide, LANES), scratch(8 * HALO, lat_cells)]
        + [scratch(tiles, wide, LANES)] * (9 * MORE),
        compiler_params=params,
        name="parareal",
    )(prepared[0], left, right, *prepared[1:])


def solution(mesh):
    return jax.shard_map(
        body,
        mesh=mesh,
        in_specs=(P(None, "lon", None), P("lon", None)),
        out_specs=P("tm", None, "lon", None),
        check_vma=False,
    )
```

```python
import math

import jax
import jax.numpy as jnp
import numpy as np
from jax import lax
from jax.experimental import pallas as pl
from jax.experimental.pallas import tpu as pltpu
from jax.sharding import PartitionSpec as P

STEPS = 3
ROUNDS = 2
LAT_LIMIT = 1.2
COURANT = 1.2
DEPTH_MAX = 1.5
GRAVITY = 1.0
TURN_RATE = 0.15

HALO = 2 * STEPS * ROUNDS
ROWS = 8
LANES = 128
DEAL_ROWS = 64
FIRST, MORE = 3, 4
VMEM_LIMIT = 24 << 20
EDGE_LIMIT = 2 << 20

EAST, POLE, DIVERGE, SPIN_U, SPIN_V, GRAD_E, GRAD_N, TURN_C, TURN_U, TURN_V, EAST_INV, POLE_INV = range(12)


def lat_table(lon_cells, lat_cells):
    latitude = -LAT_LIMIT + (np.arange(lat_cells) + 0.5) * (2.0 * LAT_LIMIT / lat_cells)
    cosine = np.cos(latitude)
    north_spacing = 2.0 * LAT_LIMIT / lat_cells
    east_spacing = cosine * (2.0 * math.pi / lon_cells)
    narrowest = math.cos(LAT_LIMIT - LAT_LIMIT / lat_cells) * 2.0 * math.pi / lon_cells
    time_step = COURANT / (
        math.sqrt(DEPTH_MAX * GRAVITY) * math.sqrt(1.0 / narrowest**2 + 1.0 / north_spacing**2)
    )
    spin = TURN_RATE * np.sin(latitude)
    turning = spin * STEPS
    east = time_step / (2.0 * east_spacing)
    north = time_step / (2.0 * north_spacing)
    rows = [None] * 12
    rows[EAST] = east
    rows[POLE] = cosine
    rows[DIVERGE] = north / cosine
    rows[SPIN_U] = spin * east / cosine
    rows[SPIN_V] = spin * cosine / east
    rows[GRAD_E] = GRAVITY * east
    rows[GRAD_N] = GRAVITY * north + 0.0 * cosine
    rows[TURN_C] = np.cos(turning)
    rows[TURN_U] = np.sin(turning) * east / cosine
    rows[TURN_V] = np.sin(turning) * cosine / east
    rows[EAST_INV] = 1.0 / east
    rows[POLE_INV] = 1.0 / cosine
    table = np.stack(rows).astype(np.float32)
    return table.reshape(12, LANES, lat_cells // LANES).swapaxes(1, 2).reshape(12, lat_cells)


def windows(low, high):
    starts = list(range(low, high - ROWS + 1, ROWS))
    if starts[-1] + ROWS < high:
        starts.append(high - ROWS)
    return starts


def deal(tiles, dealing, undealing):
    def block(index, carry):
        start = pl.multiple_of(index * DEAL_ROWS, DEAL_ROWS)
        row = start + lax.broadcasted_iota(jnp.int32, (DEAL_ROWS, LANES), 0)
        lane = lax.broadcasted_iota(jnp.int32, (DEAL_ROWS, LANES), 1)
        place = row % LANES * tiles + row // LANES
        for t in range(tiles):
            hit = row == lane * tiles + t
            dealing[pl.ds(start, DEAL_ROWS), lanes(t)] = jnp.where(hit, 1.0, 0.0).astype(jnp.bfloat16)
            hit = place == lane + t * LANES
            undealing[pl.ds(start, DEAL_ROWS), lanes(t)] = jnp.where(hit, 1.0, 0.0).astype(jnp.bfloat16)
        return carry

    lax.fori_loop(0, tiles * LANES // DEAL_ROWS, block, 0)


def times_one_hot(values, matrix):
    pieces = []
    rest = values
    for _ in range(3):
        pieces.append(rest.astype(jnp.bfloat16))
        rest = rest - pieces[-1].astype(jnp.float32)
    count = values.shape[0]
    out = jnp.dot(jnp.concatenate(pieces, axis=0), matrix, preferred_element_type=jnp.float32)
    return out[:count] + out[count : 2 * count] + out[2 * count :]


def lanes(t):
    return slice(t * LANES, (t + 1) * LANES)


def put_fields(dealt, table, tiles, count, first_row, step, refs, base):
    for t in range(tiles):
        h, u, v, d = (
            dealt[first_row + f * step : first_row + f * step + count, lanes(t)] for f in range(4)
        )
        he = d * table[EAST, :1, lanes(t)]
        hp = d * table[POLE, :1, lanes(t)]
        rows = slice(base, base + count)
        values = (h, u * he, v * hp, he * table[GRAD_E, :1, lanes(t)], hp * table[GRAD_N, :1, lanes(t)])
        for ref, value in zip(refs, values):
            ref[t, rows, :] = value


def windows(low, high):
    starts = list(range(low, high - ROWS + 1, ROWS))
    if starts[-1] + ROWS < high:
        starts.append(high - ROWS)
    return starts


def shrinking(low, high):
    return [
        (windows(low + 2 * s - 1, high - 2 * s + 1), windows(low + 2 * s, high - 2 * s))
        for s in range(1, STEPS + 1)
    ]


def strips(wide):
    offsets = range(0, HALO, ROWS)
    return [
        (
            [2 * s - 1 + k for k in offsets] + [wide - 2 * s + 1 - ROWS - k for k in offsets],
            [2 * s + k for k in offsets] + [wide - 2 * s - ROWS - k for k in offsets],
        )
        for s in range(1, STEPS + 1)
    ]


def joints(low, high):
    return [(low + 2 * s + 3, high - 2 * s - 3 - ROWS) for s in range(1, STEPS)]


def at(ref, t, row):
    return ref[t, row : row + ROWS, :]


def put(ref, t, row, value):
    ref[t, row : row + ROWS, :] = value


class Fluid:
    def __init__(self, table, tiles, grad_e, grad_n):
        lane = lax.broadcasted_iota(jnp.int32, (ROWS, LANES), 1)
        self.first, self.last = lane == 0, lane == LANES - 1
        self.table, self.tiles = table, tiles
        self.grad_e, self.grad_n = grad_e, grad_n

    def const(self, row, t):
        return self.table[row, :, lanes(t)]

    def consts(self, *rows):
        return [[self.const(row, t) for t in range(self.tiles)] for row in rows]

    def north_diff(self, parts):
        wrapped = pltpu.roll(parts[0], LANES - 1, 1)
        above = parts[1:] + [jnp.where(self.last, 0.0, wrapped)]
        wrapped = pltpu.roll(parts[-1], 1, 1)
        below = [jnp.where(self.first, 0.0, wrapped)] + parts[:-1]
        return [up - down for up, down in zip(above, below)]

    def turn(self, a, b, t):
        c = self.const(TURN_C, t)
        return c * a + self.const(TURN_U, t) * b, c * b - self.const(TURN_V, t) * a

    def fine(self, state, temps, plan, finish):
        tiles = range(self.tiles)
        for step, (height_rows, rest_rows) in enumerate(plan):
            height, alpha, beta = state
            new_h, new_a, new_b = temps[step]
            (diverge,) = self.consts(DIVERGE)
            for row in height_rows:
                flux = self.north_diff([at(beta, t, row) for t in tiles])
                for t in tiles:
                    value = at(height, t, row) - (at(alpha, t, row + 1) - at(alpha, t, row - 1))
                    put(new_h, t, row, value - diverge[t] * flux[t])
            spin_u, spin_v = self.consts(SPIN_U, SPIN_V)
            for row in rest_rows:
                here = [at(new_h, t, row) for t in tiles]
                slope = self.north_diff(here)
                for t in tiles:
                    b = at(beta, t, row)
                    east = at(new_h, t, row + 1) - at(new_h, t, row - 1)
                    a = at(alpha, t, row) + spin_u[t] * b - at(self.grad_e, t, row) * east
                    b = b - spin_v[t] * a - at(self.grad_n, t, row) * slope[t]
                    if step == STEPS - 1:
                        finish(t, row, here[t], a, b)
                    else:
                        put(new_a, t, row, a)
                        put(new_b, t, row, b)
            state = (new_h, new_a, new_b)

    def turn_rows(self, source, target, rows):
        for row in rows:
            for t in range(self.tiles):
                a, b = self.turn(at(source[0], t, row), at(source[1], t, row), t)
                put(target[0], t, row, a)
                put(target[1], t, row, b)


def stages(refs):
    return [refs[0:3], refs[3:6], (refs[6], None, None)]


def streams_of(refs):
    return [stages(refs[7 * k : 7 * k + 7]) for k in range(len(refs) // 7)]


def in_blocks(number, one_block):
    one_block(0, FIRST)

    def more(index, carry):
        one_block(FIRST + MORE * index, MORE)
        return carry

    lax.fori_loop(0, (number + MORE - FIRST - 1) // MORE, more, 0)


def cut_edges(cells, stacked, outer, inner):
    odd = lax.axis_index("lon") % 2 == 1
    for field in range(4):
        low = stacked[field * cells : field * cells + HALO, :]
        high = stacked[(field + 1) * cells - HALO : (field + 1) * cells, :]
        rows = slice(field * HALO, (field + 1) * HALO)
        outer[rows, :] = jnp.where(odd, high, low)
        inner[rows, :] = jnp.where(odd, low, high)


def prepare(cells, tiles, stacked, out, table, dealing, undealing, inner, joint, *scratch):
    number = lax.axis_index("tm")
    for row in range(table.shape[0]):
        source = stacked[4 * cells + row : 4 * cells + row + 1, :]
        table[row] = jnp.broadcast_to(source, (ROWS, tiles * LANES))
    deal(tiles, dealing, undealing)
    dealt = times_one_hot(stacked[: 4 * cells, :], dealing[...])
    put_fields(dealt, table, tiles, cells, 0, cells, [out.at[k] for k in range(5)], 0)
    for t in range(tiles):
        over = 1.0 / dealt[3 * cells :, lanes(t)]
        out[5, t] = over * table[EAST_INV, :1, lanes(t)]
        out[6, t] = over * table[POLE_INV, :1, lanes(t)]

    fluid = Fluid(table, tiles, out.at[3], out.at[4])
    reach = 2 * STEPS
    plan = shrinking(0, cells)
    guesses = [scratch[2 * k : 2 * k + 2] for k in range(MORE)]
    temps_of = streams_of(scratch[2 * MORE :])
    guesses[0][0][...] = out[1]
    guesses[0][1][...] = out[2]
    for field in range(3):
        inner[0, field, :, : cells - 2 * reach, :] = out[field, :, reach : cells - reach, :]
    every = range(0, cells, ROWS)

    def one_block(start, count):
        for k in range(count):
            one_slice(start + k, guesses[k], temps_of[k])
            fluid.turn_rows(guesses[k], guesses[(k + 1) % count], every)

    def one_slice(m, guess, temps):
        before = [inner.at[m, field] for field in range(3)]
        after = [inner.at[m + 1, field] for field in range(3)]

        def finish(t, row, h, a, b):
            own_row = row - reach
            put(after[0], t, own_row, h + (at(before[0], t, own_row) - out[0, t, row : row + ROWS, :]))
            da, db = fluid.turn(
                at(before[1], t, own_row) - at(guess[0], t, row),
                at(before[2], t, own_row) - at(guess[1], t, row),
                t,
            )
            put(after[1], t, own_row, a + da)
            put(after[2], t, own_row, b + db)

        fluid.fine((out.at[0], *guess), temps, plan, finish)
        for step, sides in enumerate(joints(0, cells)):
            for side, row in enumerate(sides):
                for field in range(3):
                    for t in range(tiles):
                        joint[m, step, side, field, t] = at(temps[step][field], t, row)

    in_blocks(number, one_block)


def kernel(cells, tiles, own, outer_halo, inner_halo, table, dealing, undealing, inner, joint, ends, *scratch):
    (s_h, grad_e, grad_n, w_h, w_a, w_b, firsts, flat) = scratch[:8]
    guesses = [scratch[8 + 2 * k : 10 + 2 * k] for k in range(MORE)]
    temps_of = streams_of(scratch[8 + 2 * MORE :])
    wide = cells + 2 * HALO
    reach = 2 * STEPS
    number = lax.axis_index("tm")
    fluid = Fluid(table, tiles, grad_e, grad_n)

    fields = (s_h, *guesses[0], grad_e, grad_n)
    odd = lax.axis_index("lon") % 2 == 1
    far, near = outer_halo[...], inner_halo[...]
    flat[: 4 * HALO, :] = jnp.where(odd, near, far)
    flat[4 * HALO :, :] = jnp.where(odd, far, near)
    dealt = times_one_hot(flat[...], dealing[...])
    put_fields(dealt, table, tiles, HALO, 0, HALO, fields, 0)
    put_fields(dealt, table, tiles, HALO, 4 * HALO, HALO, fields, HALO + cells)
    for k, ref in enumerate(fields):
        ref[:, HALO : HALO + cells, :] = own[k]
    for field, ref in enumerate(fields[:3]):
        firsts[0, field] = ref[...]

    edge_rows = [*range(0, HALO + ROWS, ROWS)]
    edge_rows = sorted({*edge_rows, *(wide - ROWS - row for row in edge_rows)})

    def round_one(m, guess, temps):
        before = [firsts.at[m, field] for field in range(3)]
        after = [firsts.at[m + 1, field] for field in range(3)]

        def finish(t, row, h, a, b):
            put(after[0], t, row, h + (at(before[0], t, row) - at(s_h, t, row)))
            da, db = fluid.turn(
                at(before[1], t, row) - at(guess[0], t, row),
                at(before[2], t, row) - at(guess[1], t, row),
                t,
            )
            put(after[1], t, row, a + da)
            put(after[2], t, row, b + db)

        for step, sides in enumerate(joints(HALO, HALO + cells)):
            for side, row in enumerate(sides):
                for field in range(3):
                    for t in range(tiles):
                        put(temps[step][field], t, row, joint[m, step, side, field, t])
        fluid.fine((s_h, *guess), temps, strips(wide), finish)
        for row in windows(0, cells - 2 * reach):
            for field in range(3):
                for t in range(tiles):
                    put(after[field], t, HALO + reach + row, at(inner.at[m + 1, field], t, row))

    def block_one(start, count):
        for k in range(count):
            round_one(start + k, guesses[k], temps_of[k])
            fluid.turn_rows(guesses[k], guesses[(k + 1) % count], edge_rows)

    def round_two(m, temps):
        first = [firsts.at[m, field] for field in range(3)]
        active = m <= number

        def finish(t, row, h, a, b):
            wh, wa, wb = (at(ref, t, row) for ref in (w_h, w_a, w_b))
            da, db = fluid.turn(wa - at(first[1], t, row), wb - at(first[2], t, row), t)
            put(w_h, t, row, jnp.where(active, h + (wh - at(first[0], t, row)), wh))
            put(w_a, t, row, jnp.where(active, a + da, wa))
            put(w_b, t, row, jnp.where(active, b + db, wb))

        fluid.fine(first, temps, shrinking(reach, wide - reach), finish)

    def block_two(start, count):
        for k in range(count):
            round_two(1 + start + k, temps_of[k])

    in_blocks(number, block_one)
    for field, ref in enumerate((w_h, w_a, w_b)):
        ref[...] = firsts[1, field]

    @pl.when(number > 0)
    def _():
        in_blocks(number, block_two)

    rows = slice(HALO, HALO + cells)
    whole = [
        jnp.concatenate([w_h[t, rows, :] for t in range(tiles)], axis=1),
        jnp.concatenate([w_a[t, rows, :] * own[5, t] for t in range(tiles)], axis=1),
        jnp.concatenate([w_b[t, rows, :] * own[6, t] for t in range(tiles)], axis=1),
    ]
    whole = times_one_hot(jnp.concatenate(whole, axis=0), undealing[...])
    for field in range(3):
        ends[0, field] = whole[field * cells : (field + 1) * cells]


def body(start, depth):
    count = lax.axis_size("lon")
    _, cells, lat_cells = start.shape
    tiles = lat_cells // LANES
    slots = FIRST + MORE * (max(lax.axis_size("tm") - 1 - FIRST + MORE - 1, 0) // MORE)
    table = jnp.asarray(lat_table(cells * count, lat_cells))
    stacked = jnp.concatenate([start.reshape(-1, lat_cells), depth, table], axis=0)
    vmem = pl.BlockSpec(memory_space=pltpu.VMEM)
    side = jax.ShapeDtypeStruct((4 * HALO, lat_cells), jnp.float32)
    outer, inner = pl.pallas_call(
        lambda *refs: cut_edges(cells, *refs),
        out_shape=(side, side),
        in_specs=[vmem],
        out_specs=[vmem] * 2,
        compiler_params=pltpu.CompilerParams(vmem_limit_bytes=EDGE_LIMIT),
        name="edges",
    )(stacked)
    ring = range(count)
    outer = lax.ppermute(outer, "lon", [(k, (k + 1 if k % 2 else k - 1) % count) for k in ring])
    inner = lax.ppermute(inner, "lon", [(k, k ^ 1) for k in ring])
    wide = cells + 2 * HALO
    inside = -(-(cells - 4 * STEPS) // ROWS) * ROWS

    def shape(*dims, dtype=jnp.float32):
        return jax.ShapeDtypeStruct(dims, dtype)

    def scratch(*dims):
        return pltpu.VMEM(dims, jnp.float32)

    params = pltpu.CompilerParams(
        vmem_limit_bytes=VMEM_LIMIT
    )
    prepared = pl.pallas_call(
        lambda *refs: prepare(cells, tiles, *refs),
        out_shape=(
            shape(7, tiles, cells, LANES),
            shape(table.shape[0], ROWS, lat_cells),
            shape(lat_cells, lat_cells, dtype=jnp.bfloat16),
            shape(lat_cells, lat_cells, dtype=jnp.bfloat16),
            shape(slots + 1, 3, tiles, inside, LANES),
            shape(slots, STEPS - 1, 2, 3, tiles, ROWS, LANES),
        ),
        in_specs=[vmem],
        out_specs=[vmem] * 6,
        scratch_shapes=[scratch(tiles, cells, LANES)] * (9 * MORE),
        compiler_params=params,
        cost_estimate=pl.CostEstimate(flops=10**9, bytes_accessed=10**7, transcendentals=0),
        name="prepare",
    )(stacked)
    return pl.pallas_call(
        lambda *refs: kernel(cells, tiles, *refs),
        out_shape=shape(1, *start.shape),
        in_specs=[vmem] * 8,
        out_specs=vmem,
        scratch_shapes=[scratch(tiles, wide, LANES)] * 6
        + [scratch(slots + 1, 3, tiles, wide, LANES), scratch(8 * HALO, lat_cells)]
        + [scratch(tiles, wide, LANES)] * (9 * MORE),
        compiler_params=params,
        name="parareal",
    )(prepared[0], outer, inner, *prepared[1:])


def solution(mesh):
    return jax.shard_map(
        body,
        mesh=mesh,
        in_specs=(P(None, "lon", None), P("lon", None)),
        out_specs=P("tm", None, "lon", None),
        check_vma=False,
    )
```

```python
import math

import jax
import jax.numpy as jnp
import numpy as np
from jax import lax
from jax.experimental import pallas as pl
from jax.experimental.pallas import tpu as pltpu
from jax.sharding import PartitionSpec as P

STEPS = 3
ROUNDS = 2
LAT_LIMIT = 1.2
COURANT = 1.2
DEPTH_MAX = 1.5
GRAVITY = 1.0
TURN_RATE = 0.15

HALO = 2 * STEPS * ROUNDS
ROWS = 8
LANES = 128
DEAL_ROWS = 64
FIRST, MORE, ABREAST = 3, 4, 7
VMEM_LIMIT = 24 << 20
EDGE_LIMIT = 2 << 20

EAST, POLE, DIVERGE, SPIN_U, SPIN_V, GRAD_E, GRAD_N, TURN_C, TURN_U, TURN_V, EAST_INV, POLE_INV = range(12)


def lat_table(lon_cells, lat_cells):
    latitude = -LAT_LIMIT + (np.arange(lat_cells) + 0.5) * (2.0 * LAT_LIMIT / lat_cells)
    cosine = np.cos(latitude)
    north_spacing = 2.0 * LAT_LIMIT / lat_cells
    east_spacing = cosine * (2.0 * math.pi / lon_cells)
    narrowest = math.cos(LAT_LIMIT - LAT_LIMIT / lat_cells) * 2.0 * math.pi / lon_cells
    time_step = COURANT / (
        math.sqrt(DEPTH_MAX * GRAVITY) * math.sqrt(1.0 / narrowest**2 + 1.0 / north_spacing**2)
    )
    spin = TURN_RATE * np.sin(latitude)
    turning = spin * STEPS
    east = time_step / (2.0 * east_spacing)
    north = time_step / (2.0 * north_spacing)
    rows = [None] * 12
    rows[EAST] = east
    rows[POLE] = cosine
    rows[DIVERGE] = north / cosine
    rows[SPIN_U] = spin * east / cosine
    rows[SPIN_V] = spin * cosine / east
    rows[GRAD_E] = GRAVITY * east
    rows[GRAD_N] = GRAVITY * north + 0.0 * cosine
    rows[TURN_C] = np.cos(turning)
    rows[TURN_U] = np.sin(turning) * east / cosine
    rows[TURN_V] = np.sin(turning) * cosine / east
    rows[EAST_INV] = 1.0 / east
    rows[POLE_INV] = 1.0 / cosine
    table = np.stack(rows).astype(np.float32)
    return table.reshape(12, LANES, lat_cells // LANES).swapaxes(1, 2).reshape(12, lat_cells)


def windows(low, high):
    starts = list(range(low, high - ROWS + 1, ROWS))
    if starts[-1] + ROWS < high:
        starts.append(high - ROWS)
    return starts


def deal(tiles, dealing, undealing):
    def block(index, carry):
        start = pl.multiple_of(index * DEAL_ROWS, DEAL_ROWS)
        row = start + lax.broadcasted_iota(jnp.int32, (DEAL_ROWS, LANES), 0)
        lane = lax.broadcasted_iota(jnp.int32, (DEAL_ROWS, LANES), 1)
        place = row % LANES * tiles + row // LANES
        for t in range(tiles):
            hit = row == lane * tiles + t
            dealing[pl.ds(start, DEAL_ROWS), lanes(t)] = jnp.where(hit, 1.0, 0.0).astype(jnp.bfloat16)
            hit = place == lane + t * LANES
            undealing[pl.ds(start, DEAL_ROWS), lanes(t)] = jnp.where(hit, 1.0, 0.0).astype(jnp.bfloat16)
        return carry

    lax.fori_loop(0, tiles * LANES // DEAL_ROWS, block, 0)


def times_one_hot(values, matrix):
    pieces = []
    rest = values
    for _ in range(3):
        pieces.append(rest.astype(jnp.bfloat16))
        rest = rest - pieces[-1].astype(jnp.float32)
    count = values.shape[0]
    out = jnp.dot(jnp.concatenate(pieces, axis=0), matrix, preferred_element_type=jnp.float32)
    return out[:count] + out[count : 2 * count] + out[2 * count :]


def lanes(t):
    return slice(t * LANES, (t + 1) * LANES)


def field_values(part, table, t):
    h, u, v, d = part
    he = d * table[EAST, :1, lanes(t)]
    hp = d * table[POLE, :1, lanes(t)]
    return h, u * he, v * hp, he * table[GRAD_E, :1, lanes(t)], hp * table[GRAD_N, :1, lanes(t)]


def windows(low, high):
    starts = list(range(low, high - ROWS + 1, ROWS))
    if starts[-1] + ROWS < high:
        starts.append(high - ROWS)
    return starts


def deal(tiles, dealing, undealing):
    def block(index, carry):
        start = pl.multiple_of(index * DEAL_ROWS, DEAL_ROWS)
        row = start + lax.broadcasted_iota(jnp.int32, (DEAL_ROWS, LANES), 0)
        lane = lax.broadcasted_iota(jnp.int32, (DEAL_ROWS, LANES), 1)
        place = row % LANES * tiles + row // LANES
        for t in range(tiles):
            hit = row == lane * tiles + t
            dealing[pl.ds(start, DEAL_ROWS), lanes(t)] = jnp.where(hit, 1.0, 0.0).astype(jnp.bfloat16)
            hit = place == lane + t * LANES
            undealing[pl.ds(start, DEAL_ROWS), lanes(t)] = jnp.where(hit, 1.0, 0.0).astype(jnp.bfloat16)
        return carry

    lax.fori_loop(0, tiles * LANES // DEAL_ROWS, block, 0)


def times_one_hot(values, matrix):
    pieces = []
    rest = values
    for _ in range(3):
        pieces.append(rest.astype(jnp.bfloat16))
        rest = rest - pieces[-1].astype(jnp.float32)
    count = values.shape[0]
    out = jnp.dot(jnp.concatenate(pieces, axis=0), matrix, preferred_element_type=jnp.float32)
    return out[:count] + out[count : 2 * count] + out[2 * count :]


def lanes(t):
    return slice(t * LANES, (t + 1) * LANES)


def put_fields(dealt, table, tiles, count, first_row, step, refs, base):
    for t in range(tiles):
        h, u, v, d = (
            dealt[first_row + f * step : first_row + f * step + count, lanes(t)] for f in range(4)
        )
        he = d * table[EAST, :1, lanes(t)]
        hp = d * table[POLE, :1, lanes(t)]
        rows = slice(base, base + count)
        values = (h, u * he, v * hp, he * table[GRAD_E, :1, lanes(t)], hp * table[GRAD_N, :1, lanes(t)])
        for ref, value in zip(refs, values):
            ref[t, rows, :] = value


def windows(low, high):
    starts = list(range(low, high - ROWS + 1, ROWS))
    if starts[-1] + ROWS < high:
        starts.append(high - ROWS)
    return starts


def shrinking(low, high):
    return [
        (windows(low + 2 * s - 1, high - 2 * s + 1), windows(low + 2 * s, high - 2 * s))
        for s in range(1, STEPS + 1)
    ]


def strip(wide, is_left):
    offsets = range(0, HALO, ROWS)

    def pick(first, k):
        return jnp.where(is_left, first + k, wide - first - ROWS - k)

    return [
        ([pick(2 * s - 1, k) for k in offsets], [pick(2 * s, k) for k in offsets])
        for s in range(1, STEPS + 1)
    ]


def joints(low, high):
    return [(low + 2 * s + 3, high - 2 * s - 3 - ROWS) for s in range(1, STEPS)]


def at(ref, t, row):
    return ref[t, pl.ds(row, ROWS), :]


def put(ref, t, row, value):
    ref[t, pl.ds(row, ROWS), :] = value


class Fluid:
    def __init__(self, table, tiles, grad_e, grad_n):
        lane = lax.broadcasted_iota(jnp.int32, (ROWS, LANES), 1)
        self.first, self.last = lane == 0, lane == LANES - 1
        self.table, self.tiles = table, tiles
        self.grad_e, self.grad_n = grad_e, grad_n

    def const(self, row, t):
        return self.table[row, :, lanes(t)]

    def consts(self, *rows):
        return [[self.const(row, t) for t in range(self.tiles)] for row in rows]

    def north_diff(self, parts):
        wrapped = pltpu.roll(parts[0], LANES - 1, 1)
        above = parts[1:] + [jnp.where(self.last, 0.0, wrapped)]
        wrapped = pltpu.roll(parts[-1], 1, 1)
        below = [jnp.where(self.first, 0.0, wrapped)] + parts[:-1]
        return [up - down for up, down in zip(above, below)]

    def turn(self, a, b, t):
        c = self.const(TURN_C, t)
        return c * a + self.const(TURN_U, t) * b, c * b - self.const(TURN_V, t) * a

    def fine(self, state, temps, plan, finish):
        tiles = range(self.tiles)
        for step, (height_rows, rest_rows) in enumerate(plan):
            height, alpha, beta = state
            new_h, new_a, new_b = temps[step]
            (diverge,) = self.consts(DIVERGE)
            for row in height_rows:
                flux = self.north_diff([at(beta, t, row) for t in tiles])
                for t in tiles:
                    value = at(height, t, row) - (at(alpha, t, row + 1) - at(alpha, t, row - 1))
                    put(new_h, t, row, value - diverge[t] * flux[t])
            spin_u, spin_v = self.consts(SPIN_U, SPIN_V)
            for index, row in enumerate(rest_rows):
                here = [at(new_h, t, row) for t in tiles]
                slope = self.north_diff(here)
                for t in tiles:
                    b = at(beta, t, row)
                    east = at(new_h, t, row + 1) - at(new_h, t, row - 1)
                    a = at(alpha, t, row) + spin_u[t] * b - at(self.grad_e, t, row) * east
                    b = b - spin_v[t] * a - at(self.grad_n, t, row) * slope[t]
                    if step == STEPS - 1:
                        finish(index, t, row, here[t], a, b)
                    else:
                        put(new_a, t, row, a)
                        put(new_b, t, row, b)
            state = (new_h, new_a, new_b)

    def next_first(self, m, firsts, out, guess, is_left=None):
        before = [firsts.at[m, field] for field in range(3)]
        after = [firsts.at[m + 1, field] for field in range(3)]
        sublane = lax.broadcasted_iota(jnp.int32, (ROWS, LANES), 0)
        spare = HALO % ROWS
        outward = None
        if is_left is not None and spare:
            outward = jnp.where(is_left, sublane, ROWS - 1 - sublane) < spare

        def finish(index, t, row, h, a, b):
            da, db = self.turn(
                at(before[1], t, row) - at(guess[0], t, row),
                at(before[2], t, row) - at(guess[1], t, row),
                t,
            )
            values = (h + (at(before[0], t, row) - at(out.at[0], t, row)), a + da, b + db)
            for ref, value in zip(after, values):
                if outward is not None and (index + 1) * ROWS > HALO:
                    value = jnp.where(outward, value, at(ref, t, row))
                put(ref, t, row, value)

        return finish

    def turn_rows(self, source, target, rows):
        for row in rows:
            for t in range(self.tiles):
                a, b = self.turn(at(source[0], t, row), at(source[1], t, row), t)
                put(target[0], t, row, a)
                put(target[1], t, row, b)


def stages(refs):
    return [refs[0:3], refs[3:6], (refs[6], None, None)]


def streams_of(refs):
    return [stages(refs[7 * k : 7 * k + 7]) for k in range(len(refs) // 7)]


def in_blocks(number, one_block, first, more):
    one_block(0, first)

    def rest(index, carry):
        one_block(first + more * index, more)
        return carry

    lax.fori_loop(0, (number + more - first - 1) // more, rest, 0)


def cut_edges(cells, stacked, outer, inner):
    odd = lax.axis_index("lon") % 2 == 1
    for field in range(4):
        low = stacked[field * cells : field * cells + HALO, :]
        high = stacked[(field + 1) * cells - HALO : (field + 1) * cells, :]
        rows = slice(field * HALO, (field + 1) * HALO)
        outer[rows, :] = jnp.where(odd, high, low)
        inner[rows, :] = jnp.where(odd, low, high)


def prepare(cells, tiles, stacked, out, scales, table, dealing, undealing, firsts, joint, *scratch):
    number = lax.axis_index("tm")
    for row in range(table.shape[0]):
        source = stacked[4 * cells + row : 4 * cells + row + 1, :]
        table[row] = jnp.broadcast_to(source, (ROWS, tiles * LANES))
    deal(tiles, dealing, undealing)
    dealt = times_one_hot(stacked[: 4 * cells, :], dealing[...])
    for t in range(tiles):
        part = [dealt[f * cells : (f + 1) * cells, lanes(t)] for f in range(4)]
        for field, value in enumerate(field_values(part, table, t)):
            out[field, t, HALO : HALO + cells, :] = value
            if field < 3:
                firsts[0, field, t, HALO : HALO + cells, :] = value
        over = 1.0 / part[3]
        scales[0, t] = over * table[EAST_INV, :1, lanes(t)]
        scales[1, t] = over * table[POLE_INV, :1, lanes(t)]

    fluid = Fluid(table, tiles, out.at[3], out.at[4])
    plan = shrinking(HALO, HALO + cells)
    guesses = [scratch[2 * k : 2 * k + 2] for k in range(MORE)]
    temps_of = streams_of(scratch[2 * MORE :])
    guesses[0][0][...] = out[1]
    guesses[0][1][...] = out[2]
    every = range(HALO, HALO + cells, ROWS)

    def one_block(start, count):
        for k in range(count):
            m, temps = start + k, temps_of[k]
            fluid.fine((out.at[0], *guesses[k]), temps, plan, fluid.next_first(m, firsts, out, guesses[k]))
            for step, sides in enumerate(joints(HALO, HALO + cells)):
                for side, row in enumerate(sides):
                    for field in range(3):
                        for t in range(tiles):
                            joint[m, step, side, field, t] = at(temps[step][field], t, row)
            fluid.turn_rows(guesses[k], guesses[(k + 1) % count], every)

    in_blocks(number, one_block, FIRST, MORE)


def one_side(cells, tiles, is_left, halo, table, dealing, out, firsts, joint, flat, guesses, temps_of):
    wide = cells + 2 * HALO
    number = lax.axis_index("tm")
    fluid = Fluid(table, tiles, out.at[3], out.at[4])
    dealt = times_one_hot(halo[...], dealing[...])
    for t in range(tiles):
        flat[t] = dealt[:, lanes(t)]
    base = jnp.where(is_left, 0, HALO + cells)
    for row in windows(0, HALO):
        for t in range(tiles):
            part = [at(flat, t, f * HALO + row) for f in range(4)]
            for field, value in enumerate(field_values(part, table, t)):
                put(out.at[field], t, base + row, value)
                if field < 3:
                    put(firsts.at[0, field], t, base + row, value)
    plan = strip(wide, is_left)
    near = [jnp.where(is_left, k, wide - ROWS - k) for k in range(0, HALO + ROWS, ROWS)]
    for row in near:
        for t in range(tiles):
            for field in range(2):
                put(guesses[0][field], t, row, at(out.at[1 + field], t, row))
    side = jnp.where(is_left, 0, 1)
    left_joints = joints(HALO, HALO + cells)

    def one_block(start, count):
        for k in range(count):
            m, temps = start + k, temps_of[k]
            for step, (row_left, row_right) in enumerate(left_joints):
                row = jnp.where(is_left, row_left, row_right)
                for field in range(3):
                    for t in range(tiles):
                        put(temps[step][field], t, row, joint[m, step, side, field, t])
            fluid.fine(
                (out.at[0], *guesses[k]), temps, plan, fluid.next_first(m, firsts, out, guesses[k], is_left)
            )
            fluid.turn_rows(guesses[k], guesses[(k + 1) % count], near)

    in_blocks(number, one_block, ABREAST, MORE)


def near_side(cells, tiles, halo, table, dealing, joint, out_in, firsts_in, out, firsts, *scratch):
    is_left = lax.axis_index("lon") % 2 == 1
    guesses = [scratch[1 + 2 * k : 3 + 2 * k] for k in range(ABREAST)]
    temps_of = streams_of(scratch[1 + 2 * ABREAST :])
    one_side(
        cells, tiles, is_left, halo, table, dealing, out, firsts, joint, scratch[0], guesses, temps_of
    )


def kernel(
    cells, tiles, halo, table, dealing, undealing, scales, joint, out_in, firsts_in,
    ends, out, firsts, *scratch,
):
    is_left = lax.axis_index("lon") % 2 == 0
    w_h, w_a, w_b = scratch[1:4]
    guesses = [scratch[4 + 2 * k : 6 + 2 * k] for k in range(ABREAST)]
    temps_of = streams_of(scratch[4 + 2 * ABREAST :])
    wide = cells + 2 * HALO
    reach = 2 * STEPS
    number = lax.axis_index("tm")
    fluid = Fluid(table, tiles, out.at[3], out.at[4])
    one_side(
        cells, tiles, is_left, halo, table, dealing, out, firsts, joint, scratch[0], guesses, temps_of
    )

    def round_two(m, temps):
        first = [firsts.at[m, field] for field in range(3)]
        active = m <= number

        def finish(step_row, t, row, h, a, b):
            wh, wa, wb = (at(ref, t, row) for ref in (w_h, w_a, w_b))
            da, db = fluid.turn(wa - at(first[1], t, row), wb - at(first[2], t, row), t)
            put(w_h, t, row, jnp.where(active, h + (wh - at(first[0], t, row)), wh))
            put(w_a, t, row, jnp.where(active, a + da, wa))
            put(w_b, t, row, jnp.where(active, b + db, wb))

        fluid.fine(first, temps, shrinking(reach, wide - reach), finish)

    def block_two(start, count):
        for k in range(count):
            round_two(1 + start + k, temps_of[k])

    for field, ref in enumerate((w_h, w_a, w_b)):
        ref[...] = firsts[1, field]

    @pl.when(number > 0)
    def _():
        in_blocks(number, block_two, FIRST, MORE)

    rows = slice(HALO, HALO + cells)
    whole = [
        jnp.concatenate([w_h[t, rows, :] for t in range(tiles)], axis=1),
        jnp.concatenate([w_a[t, rows, :] * scales[0, t] for t in range(tiles)], axis=1),
        jnp.concatenate([w_b[t, rows, :] * scales[1, t] for t in range(tiles)], axis=1),
    ]
    whole = times_one_hot(jnp.concatenate(whole, axis=0), undealing[...])
    for field in range(3):
        ends[0, field] = whole[field * cells : (field + 1) * cells]


def body(start, depth):
    count = lax.axis_size("lon")
    _, cells, lat_cells = start.shape
    tiles = lat_cells // LANES
    last = lax.axis_size("tm") - 1
    slots = max(first + MORE * max(-(-(last - first) // MORE), 0) for first in (FIRST, ABREAST))
    table = jnp.asarray(lat_table(cells * count, lat_cells))
    stacked = jnp.concatenate([start.reshape(-1, lat_cells), depth, table], axis=0)
    vmem = pl.BlockSpec(memory_space=pltpu.VMEM)
    side = jax.ShapeDtypeStruct((4 * HALO, lat_cells), jnp.float32)
    outer, inner = pl.pallas_call(
        lambda *refs: cut_edges(cells, *refs),
        out_shape=(side, side),
        in_specs=[vmem],
        out_specs=[vmem] * 2,
        compiler_params=pltpu.CompilerParams(vmem_limit_bytes=EDGE_LIMIT),
        name="edges",
    )(stacked)
    ring = range(count)
    outer = lax.ppermute(outer, "lon", [(k, (k + 1 if k % 2 else k - 1) % count) for k in ring])
    inner = lax.ppermute(inner, "lon", [(k, k ^ 1) for k in ring])
    wide = cells + 2 * HALO

    def shape(*dims, dtype=jnp.float32):
        return jax.ShapeDtypeStruct(dims, dtype)

    def scratch(*dims):
        return pltpu.VMEM(dims, jnp.float32)

    params = pltpu.CompilerParams(vmem_limit_bytes=VMEM_LIMIT)
    block = scratch(tiles, wide, LANES)
    fields = shape(5, tiles, wide, LANES)
    firsts = shape(slots + 1, 3, tiles, wide, LANES)
    halo = scratch(tiles, 4 * HALO, LANES)
    fields, scales, table, dealing, undealing, firsts, joint = pl.pallas_call(
        lambda *refs: prepare(cells, tiles, *refs),
        out_shape=(
            fields,
            shape(2, tiles, cells, LANES),
            shape(table.shape[0], ROWS, lat_cells),
            shape(lat_cells, lat_cells, dtype=jnp.bfloat16),
            shape(lat_cells, lat_cells, dtype=jnp.bfloat16),
            firsts,
            shape(slots, STEPS - 1, 2, 3, tiles, ROWS, LANES),
        ),
        in_specs=[vmem],
        out_specs=[vmem] * 7,
        scratch_shapes=[block] * (9 * MORE),
        compiler_params=params,
        cost_estimate=pl.CostEstimate(flops=10**9, bytes_accessed=10**7, transcendentals=0),
        name="prepare",
    )(stacked)
    fields, firsts = pl.pallas_call(
        lambda *refs: near_side(cells, tiles, *refs),
        out_shape=(shape(*fields.shape), shape(*firsts.shape)),
        in_specs=[vmem] * 6,
        out_specs=[vmem] * 2,
        scratch_shapes=[halo] + [block] * (9 * ABREAST),
        input_output_aliases={4: 0, 5: 1},
        compiler_params=params,
        cost_estimate=pl.CostEstimate(flops=10**9, bytes_accessed=10**7, transcendentals=0),
        name="near",
    )(inner, table, dealing, joint, fields, firsts)
    return pl.pallas_call(
        lambda *refs: kernel(cells, tiles, *refs),
        out_shape=(shape(1, *start.shape), shape(*fields.shape), shape(*firsts.shape)),
        in_specs=[vmem] * 8,
        out_specs=[vmem] * 3,
        scratch_shapes=[halo] + [block] * (3 + 9 * ABREAST),
        input_output_aliases={6: 1, 7: 2},
        compiler_params=params,
        name="parareal",
    )(outer, table, dealing, undealing, scales, joint, fields, firsts)[0]


def solution(mesh):
    return jax.shard_map(
        body,
        mesh=mesh,
        in_specs=(P(None, "lon", None), P("lon", None)),
        out_specs=P("tm", None, "lon", None),
        check_vma=False,
    )
```

```python
import math

import jax
import jax.numpy as jnp
import numpy as np
from jax import lax
from jax.experimental import pallas as pl
from jax.experimental.pallas import tpu as pltpu
from jax.sharding import PartitionSpec as P

STEPS = 3
ROUNDS = 2
LAT_LIMIT = 1.2
COURANT = 1.2
DEPTH_MAX = 1.5
GRAVITY = 1.0
TURN_RATE = 0.15

HALO = 2 * STEPS * ROUNDS
ROWS = 8
LANES = 128
DEAL_ROWS = 64
FIRST, MORE, ABREAST = 3, 4, 7
VMEM_LIMIT = 24 << 20
EDGE_LIMIT = 2 << 20

EAST, POLE, DIVERGE, SPIN_U, SPIN_V, GRAD_E, GRAD_N, TURN_C, TURN_U, TURN_V, EAST_INV, POLE_INV = range(12)


def lat_table(lon_cells, lat_cells):
    latitude = -LAT_LIMIT + (np.arange(lat_cells) + 0.5) * (2.0 * LAT_LIMIT / lat_cells)
    cosine = np.cos(latitude)
    north_spacing = 2.0 * LAT_LIMIT / lat_cells
    east_spacing = cosine * (2.0 * math.pi / lon_cells)
    narrowest = math.cos(LAT_LIMIT - LAT_LIMIT / lat_cells) * 2.0 * math.pi / lon_cells
    time_step = COURANT / (
        math.sqrt(DEPTH_MAX * GRAVITY) * math.sqrt(1.0 / narrowest**2 + 1.0 / north_spacing**2)
    )
    spin = TURN_RATE * np.sin(latitude)
    turning = spin * STEPS
    east = time_step / (2.0 * east_spacing)
    north = time_step / (2.0 * north_spacing)
    rows = [None] * 12
    rows[EAST] = east
    rows[POLE] = cosine
    rows[DIVERGE] = north / cosine
    rows[SPIN_U] = spin * east / cosine
    rows[SPIN_V] = spin * cosine / east
    rows[GRAD_E] = GRAVITY * east
    rows[GRAD_N] = GRAVITY * north + 0.0 * cosine
    rows[TURN_C] = np.cos(turning)
    rows[TURN_U] = np.sin(turning) * east / cosine
    rows[TURN_V] = np.sin(turning) * cosine / east
    rows[EAST_INV] = 1.0 / east
    rows[POLE_INV] = 1.0 / cosine
    table = np.stack(rows).astype(np.float32)
    return table.reshape(12, LANES, lat_cells // LANES).swapaxes(1, 2).reshape(12, lat_cells)


def windows(low, high):
    starts = list(range(low, high - ROWS + 1, ROWS))
    if starts[-1] + ROWS < high:
        starts.append(high - ROWS)
    return starts


def deal(tiles, dealing, undealing):
    def block(index, carry):
        start = pl.multiple_of(index * DEAL_ROWS, DEAL_ROWS)
        row = start + lax.broadcasted_iota(jnp.int32, (DEAL_ROWS, LANES), 0)
        lane = lax.broadcasted_iota(jnp.int32, (DEAL_ROWS, LANES), 1)
        there = row - lane * tiles
        tile = start // LANES
        back = (row - tile * LANES) * tiles + tile - lane
        for t in range(tiles):
            hit = jnp.where(there == t, 1.0, 0.0)
            dealing[pl.ds(start, DEAL_ROWS), lanes(t)] = hit.astype(jnp.bfloat16)
            hit = jnp.where(back == t * LANES, 1.0, 0.0)
            undealing[pl.ds(start, DEAL_ROWS), lanes(t)] = hit.astype(jnp.bfloat16)
        return carry

    lax.fori_loop(0, tiles * LANES // DEAL_ROWS, block, 0)


def times_one_hot(values, matrix):
    pieces = []
    rest = values
    for _ in range(3):
        pieces.append(rest.astype(jnp.bfloat16))
        rest = rest - pieces[-1].astype(jnp.float32)
    count = values.shape[0]
    out = jnp.dot(jnp.concatenate(pieces, axis=0), matrix, preferred_element_type=jnp.float32)
    return out[:count] + out[count : 2 * count] + out[2 * count :]


def lanes(t):
    return slice(t * LANES, (t + 1) * LANES)


def field_values(part, table, t):
    h, u, v, d = part
    he = d * table[EAST, :1, lanes(t)]
    hp = d * table[POLE, :1, lanes(t)]
    return h, u * he, v * hp, he * table[GRAD_E, :1, lanes(t)], hp * table[GRAD_N, :1, lanes(t)]


def windows(low, high):
    starts = list(range(low, high - ROWS + 1, ROWS))
    if starts[-1] + ROWS < high:
        starts.append(high - ROWS)
    return starts


def deal(tiles, dealing, undealing):
    def block(index, carry):
        start = pl.multiple_of(index * DEAL_ROWS, DEAL_ROWS)
        row = start + lax.broadcasted_iota(jnp.int32, (DEAL_ROWS, LANES), 0)
        lane = lax.broadcasted_iota(jnp.int32, (DEAL_ROWS, LANES), 1)
        place = row % LANES * tiles + row // LANES
        for t in range(tiles):
            hit = row == lane * tiles + t
            dealing[pl.ds(start, DEAL_ROWS), lanes(t)] = jnp.where(hit, 1.0, 0.0).astype(jnp.bfloat16)
            hit = place == lane + t * LANES
            undealing[pl.ds(start, DEAL_ROWS), lanes(t)] = jnp.where(hit, 1.0, 0.0).astype(jnp.bfloat16)
        return carry

    lax.fori_loop(0, tiles * LANES // DEAL_ROWS, block, 0)


def times_one_hot(values, matrix):
    pieces = []
    rest = values
    for _ in range(3):
        pieces.append(rest.astype(jnp.bfloat16))
        rest = rest - pieces[-1].astype(jnp.float32)
    count = values.shape[0]
    out = jnp.dot(jnp.concatenate(pieces, axis=0), matrix, preferred_element_type=jnp.float32)
    return out[:count] + out[count : 2 * count] + out[2 * count :]


def lanes(t):
    return slice(t * LANES, (t + 1) * LANES)


def put_fields(dealt, table, tiles, count, first_row, step, refs, base):
    for t in range(tiles):
        h, u, v, d = (
            dealt[first_row + f * step : first_row + f * step + count, lanes(t)] for f in range(4)
        )
        he = d * table[EAST, :1, lanes(t)]
        hp = d * table[POLE, :1, lanes(t)]
        rows = slice(base, base + count)
        values = (h, u * he, v * hp, he * table[GRAD_E, :1, lanes(t)], hp * table[GRAD_N, :1, lanes(t)])
        for ref, value in zip(refs, values):
            ref[t, rows, :] = value


def windows(low, high):
    starts = list(range(low, high - ROWS + 1, ROWS))
    if starts[-1] + ROWS < high:
        starts.append(high - ROWS)
    return starts


def shrinking(low, high):
    return [
        (windows(low + 2 * s - 1, high - 2 * s + 1), windows(low + 2 * s, high - 2 * s))
        for s in range(1, STEPS + 1)
    ]


def strip(wide, is_left):
    offsets = range(0, HALO, ROWS)

    def pick(first, k):
        return jnp.where(is_left, first + k, wide - first - ROWS - k)

    return [
        ([pick(2 * s - 1, k) for k in offsets], [pick(2 * s, k) for k in offsets])
        for s in range(1, STEPS + 1)
    ]


def joints(low, high):
    return [(low + 2 * s + 3, high - 2 * s - 3 - ROWS) for s in range(1, STEPS)]


def at(ref, t, row):
    return ref[t, pl.ds(row, ROWS), :]


def put(ref, t, row, value):
    ref[t, pl.ds(row, ROWS), :] = value


class Fluid:
    def __init__(self, table, tiles, grad_e, grad_n):
        lane = lax.broadcasted_iota(jnp.int32, (ROWS, LANES), 1)
        self.first, self.last = lane == 0, lane == LANES - 1
        self.table, self.tiles = table, tiles
        self.grad_e, self.grad_n = grad_e, grad_n

    def const(self, row, t):
        return self.table[row, :, lanes(t)]

    def consts(self, *rows):
        return [[self.const(row, t) for t in range(self.tiles)] for row in rows]

    def north_diff(self, parts):
        wrapped = pltpu.roll(parts[0], LANES - 1, 1)
        above = parts[1:] + [jnp.where(self.last, 0.0, wrapped)]
        wrapped = pltpu.roll(parts[-1], 1, 1)
        below = [jnp.where(self.first, 0.0, wrapped)] + parts[:-1]
        return [up - down for up, down in zip(above, below)]

    def turn(self, a, b, t):
        c = self.const(TURN_C, t)
        return c * a + self.const(TURN_U, t) * b, c * b - self.const(TURN_V, t) * a

    def fine(self, state, temps, plan, finish):
        tiles = range(self.tiles)
        for step, (height_rows, rest_rows) in enumerate(plan):
            height, alpha, beta = state
            new_h, new_a, new_b = temps[step]
            (diverge,) = self.consts(DIVERGE)
            for row in height_rows:
                flux = self.north_diff([at(beta, t, row) for t in tiles])
                for t in tiles:
                    value = at(height, t, row) - (at(alpha, t, row + 1) - at(alpha, t, row - 1))
                    put(new_h, t, row, value - diverge[t] * flux[t])
            spin_u, spin_v = self.consts(SPIN_U, SPIN_V)
            for index, row in enumerate(rest_rows):
                here = [at(new_h, t, row) for t in tiles]
                slope = self.north_diff(here)
                for t in tiles:
                    b = at(beta, t, row)
                    east = at(new_h, t, row + 1) - at(new_h, t, row - 1)
                    a = at(alpha, t, row) + spin_u[t] * b - at(self.grad_e, t, row) * east
                    b = b - spin_v[t] * a - at(self.grad_n, t, row) * slope[t]
                    if step == STEPS - 1:
                        finish(index, t, row, here[t], a, b)
                    else:
                        put(new_a, t, row, a)
                        put(new_b, t, row, b)
            state = (new_h, new_a, new_b)

    def next_first(self, m, firsts, out, guess, is_left=None):
        before = [firsts.at[m, field] for field in range(3)]
        after = [firsts.at[m + 1, field] for field in range(3)]
        sublane = lax.broadcasted_iota(jnp.int32, (ROWS, LANES), 0)
        spare = HALO % ROWS
        outward = None
        if is_left is not None and spare:
            outward = jnp.where(is_left, sublane, ROWS - 1 - sublane) < spare

        def finish(index, t, row, h, a, b):
            da, db = self.turn(
                at(before[1], t, row) - at(guess[0], t, row),
                at(before[2], t, row) - at(guess[1], t, row),
                t,
            )
            values = (h + (at(before[0], t, row) - at(out.at[0], t, row)), a + da, b + db)
            for ref, value in zip(after, values):
                if outward is not None and (index + 1) * ROWS > HALO:
                    value = jnp.where(outward, value, at(ref, t, row))
                put(ref, t, row, value)

        return finish

    def turn_rows(self, source, target, rows):
        for row in rows:
            for t in range(self.tiles):
                a, b = self.turn(at(source[0], t, row), at(source[1], t, row), t)
                put(target[0], t, row, a)
                put(target[1], t, row, b)


def stages(refs):
    return [refs[0:3], refs[3:6], (refs[6], None, None)]


def streams_of(refs):
    return [stages(refs[7 * k : 7 * k + 7]) for k in range(len(refs) // 7)]


def in_blocks(number, one_block, first, more):
    one_block(0, first)

    def rest(index, carry):
        one_block(first + more * index, more)
        return carry

    lax.fori_loop(0, (number + more - first - 1) // more, rest, 0)


def cut_edges(cells, stacked, outer, inner):
    odd = lax.axis_index("lon") % 2 == 1
    for field in range(4):
        low = stacked[field * cells : field * cells + HALO, :]
        high = stacked[(field + 1) * cells - HALO : (field + 1) * cells, :]
        rows = slice(field * HALO, (field + 1) * HALO)
        outer[rows, :] = jnp.where(odd, high, low)
        inner[rows, :] = jnp.where(odd, low, high)


def prepare(cells, tiles, stacked, out, scales, table, dealing, undealing, firsts, joint, *scratch):
    number = lax.axis_index("tm")
    for row in range(table.shape[0]):
        source = stacked[4 * cells + row : 4 * cells + row + 1, :]
        table[row] = jnp.broadcast_to(source, (ROWS, tiles * LANES))
    deal(tiles, dealing, undealing)
    dealt = times_one_hot(stacked[: 4 * cells, :], dealing[...])
    for t in range(tiles):
        part = [dealt[f * cells : (f + 1) * cells, lanes(t)] for f in range(4)]
        for field, value in enumerate(field_values(part, table, t)):
            out[field, t, HALO : HALO + cells, :] = value
            if field < 3:
                firsts[0, field, t, HALO : HALO + cells, :] = value
        over = 1.0 / part[3]
        scales[0, t] = over * table[EAST_INV, :1, lanes(t)]
        scales[1, t] = over * table[POLE_INV, :1, lanes(t)]

    fluid = Fluid(table, tiles, out.at[3], out.at[4])
    plan = shrinking(HALO, HALO + cells)
    guesses = [scratch[2 * k : 2 * k + 2] for k in range(MORE)]
    temps_of = streams_of(scratch[2 * MORE :])
    guesses[0][0][...] = out[1]
    guesses[0][1][...] = out[2]
    every = range(HALO, HALO + cells, ROWS)

    def one_block(start, count):
        for k in range(count):
            m, temps = start + k, temps_of[k]
            fluid.fine((out.at[0], *guesses[k]), temps, plan, fluid.next_first(m, firsts, out, guesses[k]))
            for step, sides in enumerate(joints(HALO, HALO + cells)):
                for side, row in enumerate(sides):
                    for field in range(3):
                        for t in range(tiles):
                            joint[m, step, side, field, t] = at(temps[step][field], t, row)
            fluid.turn_rows(guesses[k], guesses[(k + 1) % count], every)

    in_blocks(number, one_block, FIRST, MORE)


def one_side(cells, tiles, is_left, halo, table, dealing, out, firsts, joint, flat, guesses, temps_of):
    wide = cells + 2 * HALO
    number = lax.axis_index("tm")
    fluid = Fluid(table, tiles, out.at[3], out.at[4])
    dealt = times_one_hot(halo[...], dealing[...])
    for t in range(tiles):
        flat[t] = dealt[:, lanes(t)]
    base = jnp.where(is_left, 0, HALO + cells)
    for row in windows(0, HALO):
        for t in range(tiles):
            part = [at(flat, t, f * HALO + row) for f in range(4)]
            for field, value in enumerate(field_values(part, table, t)):
                put(out.at[field], t, base + row, value)
                if field < 3:
                    put(firsts.at[0, field], t, base + row, value)
    plan = strip(wide, is_left)
    near = [jnp.where(is_left, k, wide - ROWS - k) for k in range(0, HALO + ROWS, ROWS)]
    for row in near:
        for t in range(tiles):
            for field in range(2):
                put(guesses[0][field], t, row, at(out.at[1 + field], t, row))
    side = jnp.where(is_left, 0, 1)
    left_joints = joints(HALO, HALO + cells)

    def one_block(start, count):
        for k in range(count):
            m, temps = start + k, temps_of[k]
            for step, (row_left, row_right) in enumerate(left_joints):
                row = jnp.where(is_left, row_left, row_right)
                for field in range(3):
                    for t in range(tiles):
                        put(temps[step][field], t, row, joint[m, step, side, field, t])
            fluid.fine(
                (out.at[0], *guesses[k]), temps, plan, fluid.next_first(m, firsts, out, guesses[k], is_left)
            )
            fluid.turn_rows(guesses[k], guesses[(k + 1) % count], near)

    in_blocks(number, one_block, ABREAST, MORE)


def near_side(cells, tiles, halo, table, dealing, joint, out_in, firsts_in, out, firsts, *scratch):
    is_left = lax.axis_index("lon") % 2 == 1
    guesses = [scratch[1 + 2 * k : 3 + 2 * k] for k in range(ABREAST)]
    temps_of = streams_of(scratch[1 + 2 * ABREAST :])
    one_side(
        cells, tiles, is_left, halo, table, dealing, out, firsts, joint, scratch[0], guesses, temps_of
    )


def kernel(
    cells, tiles, halo, table, dealing, undealing, scales, joint, out_in, firsts_in,
    ends, out, firsts, *scratch,
):
    is_left = lax.axis_index("lon") % 2 == 0
    w_h, w_a, w_b = scratch[1:4]
    guesses = [scratch[4 + 2 * k : 6 + 2 * k] for k in range(ABREAST)]
    temps_of = streams_of(scratch[4 + 2 * ABREAST :])
    wide = cells + 2 * HALO
    reach = 2 * STEPS
    number = lax.axis_index("tm")
    fluid = Fluid(table, tiles, out.at[3], out.at[4])
    one_side(
        cells, tiles, is_left, halo, table, dealing, out, firsts, joint, scratch[0], guesses, temps_of
    )

    def round_two(m, temps):
        first = [firsts.at[m, field] for field in range(3)]
        active = m <= number

        def finish(step_row, t, row, h, a, b):
            wh, wa, wb = (at(ref, t, row) for ref in (w_h, w_a, w_b))
            da, db = fluid.turn(wa - at(first[1], t, row), wb - at(first[2], t, row), t)
            put(w_h, t, row, jnp.where(active, h + (wh - at(first[0], t, row)), wh))
            put(w_a, t, row, jnp.where(active, a + da, wa))
            put(w_b, t, row, jnp.where(active, b + db, wb))

        fluid.fine(first, temps, shrinking(reach, wide - reach), finish)

    def block_two(start, count):
        for k in range(count):
            round_two(1 + start + k, temps_of[k])

    for field, ref in enumerate((w_h, w_a, w_b)):
        ref[...] = firsts[1, field]

    @pl.when(number > 0)
    def _():
        in_blocks(number, block_two, FIRST, MORE)

    rows = slice(HALO, HALO + cells)
    whole = [
        jnp.concatenate([w_h[t, rows, :] for t in range(tiles)], axis=1),
        jnp.concatenate([w_a[t, rows, :] * scales[0, t] for t in range(tiles)], axis=1),
        jnp.concatenate([w_b[t, rows, :] * scales[1, t] for t in range(tiles)], axis=1),
    ]
    whole = times_one_hot(jnp.concatenate(whole, axis=0), undealing[...])
    for field in range(3):
        ends[0, field] = whole[field * cells : (field + 1) * cells]


def body(start, depth):
    count = lax.axis_size("lon")
    _, cells, lat_cells = start.shape
    tiles = lat_cells // LANES
    last = lax.axis_size("tm") - 1
    slots = max(first + MORE * max(-(-(last - first) // MORE), 0) for first in (FIRST, ABREAST))
    table = jnp.asarray(lat_table(cells * count, lat_cells))
    stacked = jnp.concatenate([start.reshape(-1, lat_cells), depth, table], axis=0)
    vmem = pl.BlockSpec(memory_space=pltpu.VMEM)
    side = jax.ShapeDtypeStruct((4 * HALO, lat_cells), jnp.float32)
    outer, inner = pl.pallas_call(
        lambda *refs: cut_edges(cells, *refs),
        out_shape=(side, side),
        in_specs=[vmem],
        out_specs=[vmem] * 2,
        compiler_params=pltpu.CompilerParams(vmem_limit_bytes=EDGE_LIMIT),
        name="edges",
    )(stacked)
    ring = range(count)
    outer = lax.ppermute(outer, "lon", [(k, (k + 1 if k % 2 else k - 1) % count) for k in ring])
    inner = lax.ppermute(inner, "lon", [(k, k ^ 1) for k in ring])
    wide = cells + 2 * HALO

    def shape(*dims, dtype=jnp.float32):
        return jax.ShapeDtypeStruct(dims, dtype)

    def scratch(*dims):
        return pltpu.VMEM(dims, jnp.float32)

    params = pltpu.CompilerParams(vmem_limit_bytes=VMEM_LIMIT)
    block = scratch(tiles, wide, LANES)
    fields = shape(5, tiles, wide, LANES)
    firsts = shape(slots + 1, 3, tiles, wide, LANES)
    halo = scratch(tiles, 4 * HALO, LANES)
    fields, scales, table, dealing, undealing, firsts, joint = pl.pallas_call(
        lambda *refs: prepare(cells, tiles, *refs),
        out_shape=(
            fields,
            shape(2, tiles, cells, LANES),
            shape(table.shape[0], ROWS, lat_cells),
            shape(lat_cells, lat_cells, dtype=jnp.bfloat16),
            shape(lat_cells, lat_cells, dtype=jnp.bfloat16),
            firsts,
            shape(slots, STEPS - 1, 2, 3, tiles, ROWS, LANES),
        ),
        in_specs=[vmem],
        out_specs=[vmem] * 7,
        scratch_shapes=[block] * (9 * MORE),
        compiler_params=params,
        cost_estimate=pl.CostEstimate(flops=10**9, bytes_accessed=10**7, transcendentals=0),
        name="prepare",
    )(stacked)
    fields, firsts = pl.pallas_call(
        lambda *refs: near_side(cells, tiles, *refs),
        out_shape=(shape(*fields.shape), shape(*firsts.shape)),
        in_specs=[vmem] * 6,
        out_specs=[vmem] * 2,
        scratch_shapes=[halo] + [block] * (9 * ABREAST),
        input_output_aliases={4: 0, 5: 1},
        compiler_params=params,
        cost_estimate=pl.CostEstimate(flops=10**9, bytes_accessed=10**7, transcendentals=0),
        name="near",
    )(inner, table, dealing, joint, fields, firsts)
    return pl.pallas_call(
        lambda *refs: kernel(cells, tiles, *refs),
        out_shape=(shape(1, *start.shape), shape(*fields.shape), shape(*firsts.shape)),
        in_specs=[vmem] * 8,
        out_specs=[vmem] * 3,
        scratch_shapes=[halo] + [block] * (3 + 9 * ABREAST),
        input_output_aliases={6: 1, 7: 2},
        compiler_params=params,
        name="parareal",
    )(outer, table, dealing, undealing, scales, joint, fields, firsts)[0]


def solution(mesh):
    return jax.shard_map(
        body,
        mesh=mesh,
        in_specs=(P(None, "lon", None), P("lon", None)),
        out_specs=P("tm", None, "lon", None),
        check_vma=False,
    )
```
